32 devices in a mesh: level: 4 (over x, core), dom: 8 (over z, y).
Axes of the slice: x: 2, y: 2, z: 4, core: 2. Of those that a mesh axis runs over, the one named last changes fastest.
Arguments:
- loads: float32 [4, 64, 16384], P('level', None, 'dom'), may hold values from -6 to 6
- level_blocks: bfloat16 [4, 128, 12, 128, 128], P('level', 'dom'), may hold values from -0.15625 to 0.15625
- level_cols: int32 [4, 128, 12], P('level', 'dom'), may hold values from 0 to 27, as said below
- smoother: bfloat16 [4, 128, 128, 128], P('level', 'dom'), may hold values from -0.375 to 0.375
- transfer_blocks: bfloat16 [4, 128, 8, 128, 128], P('level', 'dom'), may hold values from -0.1875 to 0.1875
- transfer_cols: int32 [4, 128, 8], P('level', 'dom'), may hold values from 0 to 15
- bound_rows: int32 [4, 8, 3, 4], P('level', 'dom'), may hold values from 0 to 15, as said below
Outputs:
- final_state: float32 [4, 64, 16384], P('level', None, 'dom')
The draws below stay inside these ranges and needn't reach their ends.
Inputs may be any that keep to these rules, and one draw needn't show every extreme that they name: `level_cols`: values below 16 name a device's own block rows; 16 + side * 4 + j names entry j of bound_rows[g, d, side]. On sections 2 and 3 a block row below 8 names only own block rows below 8 and entries j < 2; any other block row there names only own block rows from 8 on and entries j >= 2. Each list bound_rows[g, d, side] holds 4 distinct block rows of the device on that side; its first 2 entries lie below 8, the others at or above 8.
All inputs are finite; a program needn't handle non-finite values.
Results may differ from the reference program's by a relative error of at most 0.007.
Values may be sent and summed in bfloat16 or wider, within the bound.
No kernel may reach another device: no remote copies, remote signals or barrier semaphores. Data moves between devices by JAX's collectives and lax.ppermute only.
A program may use at most 64 MiB of HBM per device.

```python
import jax
import jax.numpy as jnp
from jax import lax

BS = 128
NCOL = 64
K = 12
KT = 8
HB = 4
ITERS = 2
C1 = 8
C2 = 8
S = 16
SLABS = 8
ROWS = 16384


def pick_distinct(seed_key, lead_shape, slot_count, pick_count):
    scores = jax.random.randint(seed_key, lead_shape + (slot_count,), 0, 1 << 20)
    distinct = scores * slot_count + jnp.arange(slot_count, dtype=jnp.int32)
    return lax.top_k(distinct, pick_count)[1].astype(jnp.int32)


def draw_bound_rows(key, part):
    half_width = HB // 2
    lower_rows = pick_distinct(jax.random.fold_in(key, 11), (4, SLABS, 3), C1, half_width)
    upper_rows = pick_distinct(jax.random.fold_in(key, 12), (4, SLABS, 3), C2, half_width) + C1
    return jnp.concatenate([lower_rows, upper_rows], axis=-1).astype(jnp.int32)


def draw_level_cols(key, part):
    half_width = HB // 2
    total_rows = 4 * SLABS * S
    row_index = jnp.arange(total_rows, dtype=jnp.int32)
    section = (row_index // (SLABS * S))[:, None]
    slot_index = (row_index % S)[:, None]
    raw_draw = jax.random.randint(jax.random.fold_in(key, 21), (total_rows, K), 0, 1 << 24)
    fine_pick = raw_draw % (S + 3 * HB)
    is_first = slot_index < C1
    own_count = jnp.where(is_first, C1, C2)
    coarse_pick = raw_draw % (own_count + 3 * half_width)
    beyond = coarse_pick - own_count
    side_index = beyond // half_width
    entry_index = beyond % half_width + jnp.where(is_first, 0, half_width)
    own_col = coarse_pick + jnp.where(is_first, 0, C1)
    listed_col = S + side_index * HB + entry_index
    coarse_col = jnp.where(coarse_pick < own_count, own_col, listed_col)
    columns = jnp.where(section < 2, fine_pick, coarse_col)
    return columns.reshape(4, SLABS * S, K).astype(jnp.int32)


def set_ends(values, own_key, smallest, largest):
    longest = values.shape.index(max(values.shape))
    spots = []
    for shift in (0, 1):
        where = [jax.random.randint(jax.random.fold_in(own_key, axis), (), 0, length) for axis, length in enumerate(values.shape)]
        where[longest] = (where[longest] + shift) % values.shape[longest]
        spots.append(tuple(where))
    return values.at[spots[0]].set(smallest).at[spots[1]].set(largest)


def level_of(key, dims, shards, least, largest):
    loudness, own = 1.0, jax.random.fold_in(key, 6)
    for axis_at, shards_of in shards:
        heights = jnp.exp(jax.random.uniform(jax.random.fold_in(own, axis_at), (shards_of,), jnp.float32, least / len(shards), largest / len(shards)))
        loudness = loudness * jnp.repeat(heights, dims[axis_at] // shards_of).reshape([-1 if axis == axis_at else 1 for axis in range(len(dims))])
    return loudness


def scatter_about(own_key, shape, deviation, limit, split=(), kind=jnp.bfloat16):
    values = jax.random.normal(own_key, shape, jnp.float32) * deviation
    if len(split) > 0:
        values = level_of(own_key, shape, split, -0.22, 0.18) * values
    return jnp.clip(values, min=-limit, max=limit).astype(kind)


def setup_inputs(seed: int = 0) -> dict:
    splits = jax.random.split(jax.random.key(seed), 8)
    return {
        "loads": scatter_about(splits[0], (4, NCOL, ROWS), 1.0, 6.0, ((0, 4), (2, 8)), jnp.float32),
        "level_blocks": scatter_about(splits[1], (4, SLABS * S, K, BS, BS), (K * BS) ** -0.5, 0.15625, ((0, 4), (1, 8))),
        "level_cols": draw_level_cols(jax.random.fold_in(splits[7], 71), 0),
        "smoother": scatter_about(splits[3], (4, SLABS * S, BS, BS), (2 * BS) ** -0.5, 0.375, ((0, 4), (1, 8))),
        "transfer_blocks": scatter_about(splits[4], (4, SLABS * S, KT, BS, BS), (KT * BS) ** -0.5, 0.1875, ((0, 4), (1, 8))),
        "transfer_cols": set_ends(jax.random.randint(splits[5], (4, SLABS * S, KT), 0, S), jax.random.fold_in(splits[5], 1), 0, S - 1).astype(jnp.int32),
        "bound_rows": draw_bound_rows(jax.random.fold_in(splits[7], 71), 0),
    }


def as_panels(vector):
    return vector.reshape(4, NCOL, SLABS, S, BS)


def gather_rows(source, bound_lists):
    index_rows = bound_lists[:, None, :, :, None]
    return jnp.take_along_axis(source, index_rows, axis=3)


def extend(panels, bound_rows):
    left_side = jnp.roll(panels, 1, axis=2)
    right_side = jnp.roll(panels, -1, axis=2)
    sibling = panels[jnp.array([1, 0, 3, 2])]
    return jnp.concatenate(
        [panels,
         gather_rows(left_side, bound_rows[:, :, 0]),
         gather_rows(right_side, bound_rows[:, :, 1]),
         gather_rows(sibling, bound_rows[:, :, 2])],
        axis=3)


def apply_blocks(panels, columns, blocks, groups, per_row):
    width_ext = panels.shape[3]
    flat_panels = jnp.moveaxis(panels, 1, 2).reshape(groups * SLABS, NCOL, width_ext, BS)
    flat_columns = columns.reshape(groups * SLABS, S * per_row)
    flat_blocks = blocks.reshape(groups * SLABS, S, per_row, BS, BS)

    def one_device(operands):
        panel_set, column_set, block_set = operands
        picked = jnp.take(panel_set, column_set, axis=1).reshape(NCOL, S, per_row, BS).astype(jnp.float32)
        return jnp.einsum("cskb,skab->csa", picked, block_set.astype(jnp.float32))

    result = lax.map(one_device, (flat_panels, flat_columns, flat_blocks))
    return jnp.moveaxis(result.reshape(groups, SLABS, NCOL, S, BS), 2, 1)


def smooth(panels, smoother):
    blocks = smoother.reshape(4, SLABS, S, BS, BS).astype(jnp.float32)
    return jnp.einsum("gcdsb,gdsab->gcdsa", panels.astype(jnp.float32), blocks)


def reference(loads, level_blocks, level_cols, smoother, transfer_blocks, transfer_cols, bound_rows):
    load_panels = as_panels(loads)
    fine_loads = load_panels[0:2]
    coarse_loads = load_panels[2:4]
    iterate = jnp.zeros_like(fine_loads)
    residual = fine_loads
    blank_part = jnp.zeros(coarse_loads.shape, jnp.bfloat16)
    correction = jnp.zeros_like(load_panels)
    for cycle_index in range(ITERS):
        if cycle_index > 0:
            rounded = jnp.concatenate([iterate.astype(jnp.bfloat16), blank_part], axis=0)
            product = apply_blocks(extend(rounded, bound_rows), level_cols, level_blocks, 4, K)
            residual = fine_loads - product[0:2]
        residual_b = residual.astype(jnp.bfloat16)
        restricted = coarse_loads + apply_blocks(residual_b, transfer_cols[2:4], transfer_blocks[2:4], 2, KT)
        current = jnp.concatenate([residual, restricted], axis=0)
        first_step = smooth(current.astype(jnp.bfloat16), smoother).astype(jnp.bfloat16)
        applied = apply_blocks(extend(first_step, bound_rows), level_cols, level_blocks, 4, K)
        second_in = (current - applied).astype(jnp.bfloat16)
        correction = first_step.astype(jnp.float32) + smooth(second_in, smoother)
        coarse_b = correction[2:4].astype(jnp.bfloat16)
        iterate = iterate + correction[0:2] + apply_blocks(coarse_b, transfer_cols[0:2], transfer_blocks[0:2], 2, KT)
    final_state = jnp.concatenate([iterate, correction[2:4]], axis=0)
    return final_state.reshape(4, NCOL, SLABS * S * BS)
```

```python
import jax
import jax.numpy as jnp
from jax import lax
from jax.experimental import pallas as pl
from jax.experimental.pallas import tpu as pltpu
from jax.sharding import PartitionSpec as P

ITERS = 2
VMEM = pl.BlockSpec(memory_space=pltpu.VMEM)
SMEM = pl.BlockSpec(memory_space=pltpu.SMEM)
NT = (((1,), (1,)), ((), ()))


def partner(x, axis, apart):
    return lax.ppermute(x, axis, [(i, i ^ 1 << apart) for i in range(lax.axis_size(axis))])


def passed_along(value, axis, steps):
    count = lax.axis_size(axis)
    pairs = [(source, (source + steps) % count) for source in range(count)]
    return lax.ppermute(value, axis, pairs)


def from_behind(x, axis, by):
    size = lax.axis_size(axis)
    pairs = [(i, i + by) for i in range(size) if 0 <= i + by < size]
    return lax.ppermute(x, axis, pairs)


def times(panel, block):
    return lax.dot_general(panel, block, NT, preferred_element_type=jnp.float32)


def gathered(source, table, row, base, blocks):
    count = blocks.shape[1]
    left = jnp.concatenate([source[table[base + row * count + k]] for k in range(count)], axis=1)
    right = jnp.concatenate([blocks[row, k] for k in range(count)], axis=1)
    return times(left, right)


def packed(source, table, base, outs):
    for side, out in enumerate(outs):
        for j in range(out.shape[0]):
            out[j] = source[table[base + side * out.shape[0] + j]]


def first_body(where, table, loads, residual, arrived, transfer, smoother, current, first, *outs):
    rows, _, width = first.shape

    def step(i, value):
        current[i] = value
        first[i] = times(value.astype(jnp.bfloat16), smoother[i]).astype(jnp.bfloat16)

    @pl.when(table[where["fine"]] == 1)
    def _():
        for i in range(rows):
            step(i, residual[i])

    @pl.when(table[where["fine"]] == 0)
    def _():
        for i in range(rows):
            load = loads[:, i * width : (i + 1) * width]
            step(i, load + gathered(arrived, table, i, where["transfer"], transfer))

    packed(first, table, where["wanted"], outs)


def extended(own, sides, scratch):
    rows = own.shape[0]
    for i in range(rows):
        scratch[i] = own[i]
    for side, ref in enumerate(sides):
        for j in range(ref.shape[0]):
            scratch[rows + side * ref.shape[0] + j] = ref[j]


def second_body(where, table, current, first, left, right, sibling, blocks, smoother, full, rounded, scratch):
    extended(first, (left, right, sibling), scratch)
    for i in range(first.shape[0]):
        applied = gathered(scratch, table, i, where["level"], blocks)
        second = (current[i] - applied).astype(jnp.bfloat16)
        value = first[i].astype(jnp.float32) + times(second, smoother[i])
        full[i] = value
        rounded[i] = value.astype(jnp.bfloat16)


def update_body(where, table, correction, arrived, transfer, iterate, rounded, *outs):
    @pl.when(table[where["fine"]] == 1)
    def _():
        for i in range(iterate.shape[0]):
            value = correction[i] + gathered(arrived, table, i, where["transfer"], transfer)
            iterate[i] = value
            rounded[i] = value.astype(jnp.bfloat16)
        packed(rounded, table, where["wanted"], outs)


def residual_body(where, table, loads, rounded, left, right, sibling, blocks, residual, sent, scratch):
    @pl.when(table[where["fine"]] == 1)
    def _():
        width = residual.shape[2]
        extended(rounded, (left, right, sibling), scratch)
        for i in range(residual.shape[0]):
            load = loads[:, i * width : (i + 1) * width]
            value = load - gathered(scratch, table, i, where["level"], blocks)
            residual[i] = value
            sent[i] = value.astype(jnp.bfloat16)


def last_body(where, table, iterate, correction, arrived, transfer, out):
    width = correction.shape[2]

    @pl.when(table[where["fine"]] == 1)
    def _():
        for i in range(correction.shape[0]):
            value = iterate[i] + correction[i]
            value = value + gathered(arrived, table, i, where["transfer"], transfer)
            out[:, i * width : (i + 1) * width] = value

    @pl.when(table[where["fine"]] == 0)
    def _():
        for i in range(correction.shape[0]):
            out[:, i * width : (i + 1) * width] = correction[i]


def local(loads, level_blocks, level_cols, smoother, transfer_blocks, transfer_cols, bound_rows):
    block_rows, level_count = level_cols.shape[1:]
    width = level_blocks.shape[-1]
    load_cols = loads.shape[1]
    list_width = bound_rows.shape[-1]
    transfer_count = transfer_cols.shape[-1]
    section_fine = lax.axis_index("level") < 2
    bound_lists = bound_rows[0, 0]
    blocks, smooth, transfer, loads = level_blocks[0], smoother[0], transfer_blocks[0], loads[0]

    load_panels = loads.reshape(load_cols, block_rows, width).transpose(1, 0, 2)
    sent = load_panels.astype(jnp.bfloat16)
    arrived = from_behind(sent, "level", 2)

    wanted = (
        passed_along(bound_lists[0], "dom", -1),
        passed_along(bound_lists[1], "dom", 1),
        partner(bound_lists[2], "level", 0),
    )
    fine = section_fine.astype(jnp.int32).reshape(1)
    parts = {
        "fine": fine,
        "level": level_cols.reshape(-1),
        "transfer": transfer_cols.reshape(-1),
        "wanted": jnp.concatenate(wanted),
    }
    where, at = {}, 0
    for name, part in parts.items():
        where[name] = at
        at += part.shape[0]
    table = jnp.concatenate(list(parts.values()))

    panels = (block_rows, load_cols, width)
    wide = jax.ShapeDtypeStruct(panels, jnp.float32)
    narrow = jax.ShapeDtypeStruct(panels, jnp.bfloat16)
    listed = jax.ShapeDtypeStruct((list_width, load_cols, width), jnp.bfloat16)
    extension = pltpu.VMEM((block_rows + 3 * list_width, load_cols, width), jnp.bfloat16)

    def run(body, outs, *args, scratch=(), name=None):
        def kernel(*refs):
            body(where, *refs)

        return pl.pallas_call(
            kernel,
            out_shape=outs,
            in_specs=[SMEM] + [VMEM] * len(args),
            out_specs=jax.tree.map(lambda _: VMEM, outs),
            scratch_shapes=list(scratch),
            name=name,
            compiler_params=pltpu.CompilerParams(vmem_limit_bytes=24 << 20),
        )(table, *args)

    def exchanged(packs):
        to_right, to_left, to_sibling = packs
        return (
            passed_along(to_right, "dom", 1),
            passed_along(to_left, "dom", -1),
            partner(to_sibling, "level", 0),
        )

    residual = load_panels
    iterate = None
    for cycle_index in range(ITERS):
        if cycle_index > 0:
            residual, sent = run(
                residual_body, (wide, narrow), loads, rounded, *sides, blocks,
                scratch=[extension], name="residual",
            )
            arrived = from_behind(sent, "level", 2)
        current, first, *packs = run(
            first_body, (wide, narrow, listed, listed, listed),
            loads, residual, arrived, transfer, smooth, name="first",
        )
        correction, rounded = run(
            second_body, (wide, narrow), current, first, *exchanged(packs), blocks, smooth,
            scratch=[extension], name="second",
        )
        returned = from_behind(rounded, "level", -2)
        if cycle_index + 1 < ITERS:
            if iterate is not None:
                correction = iterate + correction
            iterate, rounded, *packs = run(
                update_body, (wide, narrow, listed, listed, listed),
                correction, returned, transfer, name="update",
            )
            sides = exchanged(packs)
    out = jax.ShapeDtypeStruct((load_cols, block_rows * width), jnp.float32)
    final = run(last_body, out, iterate, correction, returned, transfer, name="last")
    return final[None]


def solution(mesh):
    in_specs = (
        P("level", None, "dom"),
        P("level", "dom", None, None, None),
        P("level", "dom", None),
        P("level", "dom", None, None),
        P("level", "dom", None, None, None),
        P("level", "dom", None),
        P("level", "dom", None, None),
    )
    out_specs = P("level", None, "dom")
    return jax.shard_map(local, mesh=mesh, in_specs=in_specs, out_specs=out_specs, check_vma=False)
```

```python
import functools

import jax
import jax.numpy as jnp
from jax import lax
from jax.experimental import pallas as pl
from jax.experimental.pallas import tpu as pltpu
from jax.sharding import PartitionSpec as P

ITERS = 2
CHUNK = 4
LIMIT = 16 << 20
VMEM = pl.BlockSpec(memory_space=pltpu.VMEM)
SMEM = pl.BlockSpec(memory_space=pltpu.SMEM)
HBM = pl.BlockSpec(memory_space=pltpu.HBM)
NT = (((1,), (1,)), ((), ()))


def partner(x, axis, apart):
    return lax.ppermute(x, axis, [(i, i ^ 1 << apart) for i in range(lax.axis_size(axis))])


def passed_along(value, axis, steps):
    count = lax.axis_size(axis)
    pairs = [(source, (source + steps) % count) for source in range(count)]
    return lax.ppermute(value, axis, pairs)


def like(x):
    return jax.ShapeDtypeStruct(x.shape, x.dtype)


def times(panel, block):
    return lax.dot_general(panel, block, NT, preferred_element_type=jnp.float32)


def gathered(source, table, row, base, blocks):
    count = blocks.shape[1]
    left = jnp.concatenate([source[table[base + row * count + k]] for k in range(count)], axis=1)
    right = jnp.concatenate([blocks[row, k] for k in range(count)], axis=1)
    return times(left, right)


def packed(source, table, base, outs):
    for side, out in enumerate(outs):
        for j in range(out.shape[0]):
            out[j] = source[table[base + side * out.shape[0] + j]]


def open_body(loads, panels, sent, arrivals):
    rows, _, width = panels.shape

    def copy(i):
        return pltpu.make_async_copy(
            loads.at[:, pl.ds(i * width, width)], panels.at[i], arrivals.at[i]
        )

    for i in range(rows):
        copy(i).start()
    for i in range(rows):
        copy(i).wait()
        sent[i] = panels[i].astype(jnp.bfloat16)


def fetched(source, target, arrivals):
    return [
        pltpu.make_async_copy(source.at[i], target.at[i], arrivals.at[i])
        for i in range(source.shape[0])
    ]


def first_body(fetch, where, table, loads, residual, arrived, transfer, smoother, current, first, *rest):
    rows = first.shape[0]
    if fetch:
        outs, (kept, kept_smoother, arrivals, smoother_arrivals) = rest[:-4], rest[-4:]
        copies = fetched(transfer, kept, arrivals)
        smoother_copies = fetched(smoother, kept_smoother, smoother_arrivals)
        for copy in copies + smoother_copies:
            copy.start()
        transfer, smoother = kept, kept_smoother
    else:
        outs = rest

    @pl.when(table[where["fine"]] == 1)
    def _():
        for i in range(rows):
            current[i] = residual[i]
            if fetch:
                copies[i].wait()

    @pl.when(table[where["fine"]] == 0)
    def _():
        for i in range(rows):
            if fetch and i % CHUNK == 0:
                for copy in copies[i : i + CHUNK]:
                    copy.wait()
            added = gathered(arrived, table, i, where["transfer"], transfer)
            current[i] = loads[i] + added

    if fetch:
        for copy in smoother_copies:
            copy.wait()
    for i in range(rows):
        value = times(current[i].astype(jnp.bfloat16), smoother[i])
        first[i] = value.astype(jnp.bfloat16)
    packed(first, table, where["wanted"], outs)


def extended(own, sides, scratch):
    rows = own.shape[0]
    for i in range(rows):
        scratch[i] = own[i]
    for side, ref in enumerate(sides):
        for j in range(ref.shape[0]):
            scratch[rows + side * ref.shape[0] + j] = ref[j]


def second_body(fetch, where, table, current, first, left, right, sibling, blocks, smoother, full, rounded, *rest):
    if fetch:
        kept, scratch, arrivals = rest
        copies = fetched(blocks, kept, arrivals)
        for copy in copies:
            copy.start()
        blocks = kept
    else:
        scratch = rest[0]
    extended(first, (left, right, sibling), scratch)
    for i in range(first.shape[0]):
        if fetch and i % CHUNK == 0:
            for copy in copies[i : i + CHUNK]:
                copy.wait()
        applied = gathered(scratch, table, i, where["level"], blocks)
        rounded[i] = (current[i] - applied).astype(jnp.bfloat16)
    for i in range(first.shape[0]):
        value = first[i].astype(jnp.float32) + times(rounded[i], smoother[i])
        full[i] = value
        rounded[i] = value.astype(jnp.bfloat16)


def update_body(where, table, correction, arrived, transfer, iterate, rounded, *outs):
    @pl.when(table[where["fine"]] == 1)
    def _():
        for i in range(iterate.shape[0]):
            added = gathered(arrived, table, i, where["transfer"], transfer)
            value = correction[i] + added
            iterate[i] = value
            rounded[i] = value.astype(jnp.bfloat16)
        packed(rounded, table, where["wanted"], outs)


def residual_body(where, table, loads, rounded, left, right, sibling, blocks, residual, sent, scratch):
    @pl.when(table[where["fine"]] == 1)
    def _():
        extended(rounded, (left, right, sibling), scratch)
        for i in range(residual.shape[0]):
            value = loads[i] - gathered(scratch, table, i, where["level"], blocks)
            residual[i] = value
            sent[i] = value.astype(jnp.bfloat16)


def last_body(where, table, iterate, correction, arrived, transfer, out, total, leaves):
    rows, _, width = correction.shape

    def copy(i):
        return pltpu.make_async_copy(total.at[i], out.at[:, pl.ds(i * width, width)], leaves.at[i])

    @pl.when(table[where["fine"]] == 1)
    def _():
        for i in range(rows):
            added = gathered(arrived, table, i, where["transfer"], transfer)
            total[i] = (iterate[i] + correction[i]) + added
            copy(i).start()

    @pl.when(table[where["fine"]] == 0)
    def _():
        for i in range(rows):
            total[i] = correction[i]
            copy(i).start()

    for i in range(rows):
        copy(i).wait()


def local(loads, level_blocks, level_cols, smoother, transfer_blocks, transfer_cols, bound_rows):
    block_rows, level_count = level_cols.shape[1:]
    width = level_blocks.shape[-1]
    load_cols = loads.shape[1]
    list_width = bound_rows.shape[-1]
    transfer_count = transfer_cols.shape[-1]
    section_fine = lax.axis_index("level") < 2
    bound_lists = bound_rows[0, 0]
    blocks, smooth, transfer, loads = level_blocks[0], smoother[0], transfer_blocks[0], loads[0]

    panels = (block_rows, load_cols, width)
    wide = jax.ShapeDtypeStruct(panels, jnp.float32)
    narrow = jax.ShapeDtypeStruct(panels, jnp.bfloat16)
    load_panels, sent = pl.pallas_call(
        open_body,
        out_shape=(wide, narrow),
        in_specs=[HBM],
        out_specs=(VMEM, VMEM),
        scratch_shapes=[pltpu.SemaphoreType.DMA((block_rows,))],
        name="open",
        cost_estimate=pl.CostEstimate(flops=0, bytes_accessed=30 << 20, transcendentals=0),
        compiler_params=pltpu.CompilerParams(vmem_limit_bytes=LIMIT),
    )(pltpu.with_memory_space_constraint(loads, pltpu.HBM))
    arrived = partner(sent, "level", 1)

    wanted = (
        passed_along(bound_lists[0], "dom", -1),
        passed_along(bound_lists[1], "dom", 1),
        partner(bound_lists[2], "level", 0),
    )
    fine = section_fine.astype(jnp.int32).reshape(1)
    parts = {
        "fine": fine,
        "level": level_cols.reshape(-1),
        "transfer": transfer_cols.reshape(-1),
        "wanted": jnp.concatenate(wanted),
    }
    where, at = {}, 0
    for name, part in parts.items():
        where[name] = at
        at += part.shape[0]
    table = jnp.concatenate(list(parts.values()))

    listed = jax.ShapeDtypeStruct((list_width, load_cols, width), jnp.bfloat16)
    rowwise = pltpu.SemaphoreType.DMA((block_rows,))
    extension = pltpu.VMEM((block_rows + 3 * list_width, load_cols, width), jnp.bfloat16)

    def run(body, outs, *args, here=(), out_specs=None, scratch=(), name=None):
        def kernel(*refs):
            body(where, *refs)

        args = [
            pltpu.with_memory_space_constraint(x, pltpu.HBM) if i in here else x
            for i, x in enumerate(args)
        ]

        return pl.pallas_call(
            kernel,
            out_shape=outs,
            in_specs=[SMEM] + [HBM if i in here else VMEM for i in range(len(args))],
            out_specs=out_specs or jax.tree.map(lambda _: VMEM, outs),
            scratch_shapes=list(scratch),
            name=name,
            compiler_params=pltpu.CompilerParams(vmem_limit_bytes=LIMIT),
        )(table, *args)

    def exchanged(packs):
        to_right, to_left, to_sibling = packs
        return (
            passed_along(to_right, "dom", 1),
            passed_along(to_left, "dom", -1),
            partner(to_sibling, "level", 0),
        )

    residual = load_panels
    iterate = None
    for cycle_index in range(ITERS):
        if cycle_index > 0:
            residual, sent = run(
                residual_body, (wide, narrow), load_panels, rounded, *sides, blocks,
                scratch=[extension], name="residual",
            )
            arrived = partner(sent, "level", 1)
        fetch = cycle_index == 0
        outs = (wide, narrow, listed, listed, listed)
        args = (load_panels, residual, arrived, transfer, smooth)
        body = functools.partial(first_body, fetch)
        if fetch:
            current, first, *packs, transfer, smooth = run(
                body, outs + (like(transfer), like(smooth)),
                *args, here=(3, 4), scratch=[rowwise, rowwise], name="first",
            )
        else:
            current, first, *packs = run(body, outs, *args, name="first")
        args = (current, first, *exchanged(packs), blocks, smooth)
        body = functools.partial(second_body, fetch)
        if fetch:
            correction, rounded, blocks = run(
                body, (wide, narrow, like(blocks)), *args, here=(5,),
                scratch=[extension, rowwise], name="second",
            )
        else:
            correction, rounded = run(body, (wide, narrow), *args, scratch=[extension], name="second")
        returned = partner(rounded, "level", 1)
        if cycle_index + 1 < ITERS:
            if iterate is not None:
                correction = iterate + correction
            iterate, rounded, *packs = run(
                update_body, (wide, narrow, listed, listed, listed),
                correction, returned, transfer, name="update",
            )
            sides = exchanged(packs)
    final = run(
        last_body, jax.ShapeDtypeStruct((load_cols, block_rows * width), jnp.float32),
        iterate, correction, returned, transfer, out_specs=HBM,
        scratch=[pltpu.VMEM(panels, jnp.float32), pltpu.SemaphoreType.DMA((block_rows,))], name="last",
    )
    return final[None]


def solution(mesh):
    in_specs = (
        P("level", None, "dom"),
        P("level", "dom", None, None, None),
        P("level", "dom", None),
        P("level", "dom", None, None),
        P("level", "dom", None, None, None),
        P("level", "dom", None),
        P("level", "dom", None, None),
    )
    out_specs = P("level", None, "dom")
    return jax.shard_map(local, mesh=mesh, in_specs=in_specs, out_specs=out_specs, check_vma=False)
```

```python
import jax
import jax.numpy as jnp
from jax import lax
from jax.experimental import pallas as pl
from jax.experimental.pallas import tpu as pltpu
from jax.sharding import PartitionSpec as P

ITERS = 2
PARTS = 2
LIMIT = 16 << 20
LANES = 128
VMEM = pl.BlockSpec(memory_space=pltpu.VMEM)
HBM = pl.BlockSpec(memory_space=pltpu.HBM)
NT = (((1,), (1,)), ((), ()))


def partner(x, axis, apart):
    return lax.ppermute(x, axis, [(i, i ^ 1 << apart) for i in range(lax.axis_size(axis))])


def swapped(x, axis, first):
    size = lax.axis_size(axis)
    pairs = [(i % size, (i + 1) % size) for i in range(first, first + size, 2)]
    return lax.ppermute(x, axis, pairs + [(b, a) for a, b in pairs])


def like(x):
    return jax.ShapeDtypeStruct(x.shape, x.dtype)


def inside(x):
    return pltpu.with_memory_space_constraint(x, pltpu.HBM)


def call(body, outs, *args, in_specs=None, out_specs=None, scratch=(), cost=None):
    if cost is None:
        size = sum(x.size * x.dtype.itemsize for x in (*args, *jax.tree.leaves(outs)))
        cost = pl.CostEstimate(flops=64 * size, bytes_accessed=size, transcendentals=0)
    return pl.pallas_call(
        body,
        out_shape=outs,
        in_specs=in_specs or [VMEM] * len(args),
        out_specs=out_specs or jax.tree.map(lambda _: VMEM, outs),
        scratch_shapes=list(scratch),
        cost_estimate=cost,
        compiler_params=pltpu.CompilerParams(vmem_limit_bytes=LIMIT),
    )(*args)


def entry(table, at):
    return table[at : at + 1, 0:1][0, 0]


def is_fine(table):
    return entry(table, table.shape[0] - 1) == 1


def times(panel, block):
    return lax.dot_general(panel, block, NT, preferred_element_type=jnp.float32)


def gathered(source, table, row, blocks):
    count = blocks.shape[1]
    left = jnp.concatenate([source[entry(table, row * count + k)] for k in range(count)], axis=1)
    right = jnp.concatenate([blocks[row, k] for k in range(count)], axis=1)
    return times(left, right)


def joined(parts, scratch):
    at = 0
    for part in parts:
        for i in range(part.shape[0]):
            scratch[at + i] = part[i]
        at += part.shape[0]


def open_body(loads, panels, sent, arrivals):
    rows, _, width = panels.shape
    copies = [
        pltpu.make_async_copy(
            loads.at[:, pl.ds(i * width, width)], panels.at[i], arrivals.at[i]
        )
        for i in range(rows)
    ]
    for copy in copies:
        copy.start()
    for i, copy in enumerate(copies):
        copy.wait()
        sent[i] = panels[i].astype(jnp.bfloat16)


def fetch_body(*refs):
    count = (len(refs) - 1) // 3
    sources, targets, arrivals = refs[1 : 1 + count], refs[1 + count : 1 + 2 * count], refs[1 + 2 * count :]
    copies = [
        pltpu.make_async_copy(source.at[i], target.at[i], arrival.at[i])
        for source, target, arrival in zip(sources, targets, arrivals)
        for i in range(source.shape[0])
    ]
    for copy in copies:
        copy.start()
    for copy in copies:
        copy.wait()


def pack_body(table, source, *outs):
    for side, out in enumerate(outs):
        for j in range(out.shape[0]):
            out[j] = source[entry(table, side * out.shape[0] + j)]


def first_body(table, loads, *refs):
    *pieces, transfer, smoother, current, first, scratch = refs
    residual, arrived = pieces[: len(pieces) // 2], pieces[len(pieces) // 2 :]
    rows = first.shape[0]

    @pl.when(is_fine(table))
    def _():
        joined(residual, current)

    @pl.when(jnp.logical_not(is_fine(table)))
    def _():
        joined(arrived, scratch)
        for i in range(rows):
            current[i] = loads[i] + gathered(scratch, table, i, transfer)

    for i in range(rows):
        value = times(current[i].astype(jnp.bfloat16), smoother[i])
        first[i] = value.astype(jnp.bfloat16)


def second_body(part, table, current, first, *refs):
    *sources, blocks, smoother, full, rounded = refs[: len(refs) - (part == 0)]
    if part == 0:
        extension = refs[-1]
        joined([first, *sources], extension)
    else:
        (extension,) = sources
    rows = full.shape[0]
    low = part * rows
    for i in range(rows):
        applied = gathered(extension, table, low + i, blocks)
        rounded[i] = (current[low + i] - applied).astype(jnp.bfloat16)
    for i in range(rows):
        value = first[low + i].astype(jnp.float32) + times(rounded[i], smoother[low + i])
        full[i] = value
        rounded[i] = value.astype(jnp.bfloat16)


def update_body(table, *refs):
    *pieces, transfer, iterate, rounded, scratch = refs
    arrived, terms = pieces[:PARTS], pieces[PARTS:]

    @pl.when(is_fine(table))
    def _():
        joined(arrived, scratch)
        rows = terms[0].shape[0]
        for i in range(iterate.shape[0]):
            value = gathered(scratch, table, i, transfer)
            for at in range(0, len(terms), PARTS):
                value = terms[at + i // rows][i % rows] + value
            iterate[i] = value
            rounded[i] = value.astype(jnp.bfloat16)


def residual_body(part, table, loads, *refs):
    *sources, blocks, residual, sent = refs[: len(refs) - (part == 0)]

    @pl.when(is_fine(table))
    def _():
        if part == 0:
            extension = refs[-1]
            joined(sources, extension)
        else:
            (extension,) = sources
        rows = residual.shape[0]
        low = part * rows
        for i in range(rows):
            value = loads[low + i] - gathered(extension, table, low + i, blocks)
            residual[i] = value
            sent[i] = value.astype(jnp.bfloat16)


def last_body(table, *refs):
    *pieces, iterate, transfer, out, total, scratch, leaves = refs
    arrived, correction = pieces[:PARTS], pieces[PARTS:]
    rows, _, width = total.shape
    piece = correction[0].shape[0]
    copies = [
        pltpu.make_async_copy(total.at[i], out.at[:, pl.ds(i * width, width)], leaves.at[i])
        for i in range(rows)
    ]

    @pl.when(is_fine(table))
    def _():
        joined(arrived, scratch)
        for i in range(rows):
            value = iterate[i] + correction[i // piece][i % piece]
            total[i] = value + gathered(scratch, table, i, transfer)
            copies[i].start()

    @pl.when(jnp.logical_not(is_fine(table)))
    def _():
        for i in range(rows):
            total[i] = correction[i // piece][i % piece]
            copies[i].start()

    for copy in copies:
        copy.wait()


def local(loads, level_blocks, level_cols, smoother, transfer_blocks, transfer_cols, bound_rows):
    block_rows = level_cols.shape[1]
    width = level_blocks.shape[-1]
    load_cols = loads.shape[1]
    list_width = bound_rows.shape[-1]
    left_list, right_list, sibling_list = bound_rows[0, 0]
    blocks, smooth, transfer, loads = level_blocks[0], smoother[0], transfer_blocks[0], loads[0]

    def panels(count, kind):
        return jax.ShapeDtypeStruct((count, load_cols, width), kind)

    def held(count):
        return pltpu.VMEM((count, load_cols, width), jnp.bfloat16)

    wide, narrow = panels(block_rows, jnp.float32), panels(block_rows, jnp.bfloat16)
    wide_part = panels(block_rows // PARTS, jnp.float32)
    narrow_part = panels(block_rows // PARTS, jnp.bfloat16)
    listed = panels(list_width, jnp.bfloat16)
    extended = panels(block_rows + 3 * list_width, jnp.bfloat16)
    rowwise = pltpu.SemaphoreType.DMA((block_rows,))

    load_panels, sent = call(
        open_body, (wide, narrow), inside(loads), in_specs=[HBM], scratch=[rowwise]
    )
    arrived = [partner(sent, "level", 1)]

    even = lax.axis_index("dom") % 2 == 0
    ahead = swapped(jnp.where(even, right_list, left_list), "dom", 0)
    behind = swapped(jnp.where(even, left_list, right_list), "dom", 1)
    wanted = jnp.concatenate([ahead, behind, partner(sibling_list, "level", 0)])
    columns = level_cols.reshape(-1)
    from_left = (columns >= block_rows) & (columns < block_rows + list_width)
    from_right = (columns >= block_rows + list_width) & (columns < block_rows + 2 * list_width)
    moved = jnp.where(from_left, list_width, 0) - jnp.where(from_right, list_width, 0)
    columns = columns + jnp.where(even, moved, 0)
    fine = (lax.axis_index("level") < 2).astype(jnp.int32).reshape(1)

    def spread(values):
        return jnp.broadcast_to(values[:, None], (values.shape[0], LANES))

    level_table = spread(jnp.concatenate([columns, fine]))
    transfer_table = spread(jnp.concatenate([transfer_cols.reshape(-1), fine]))
    wanted_table = spread(wanted)

    def fetched(after, *sources):
        size = sum(x.size * x.dtype.itemsize for x in sources)
        return call(
            fetch_body, tuple(like(x) for x in sources), inside(after), *[inside(x) for x in sources],
            in_specs=[HBM] * (1 + len(sources)), scratch=[rowwise] * len(sources),
            cost=pl.CostEstimate(flops=0, bytes_accessed=2 * size, transcendentals=0),
        )

    def exchanged(source):
        ahead, behind, beside = call(pack_body, (listed,) * 3, wanted_table, source)
        ahead = swapped(ahead, "dom", 0)
        behind = swapped(behind, "dom", 1)
        return ahead, behind, partner(beside, "level", 0)

    def in_parts(body, args, sources, rest):
        fulls, passed = [], []
        for part in range(PARTS):
            outs = (wide_part, narrow_part) + ((extended,) if part == 0 else ())
            full, rounded, *more = call(
                lambda *refs, part=part: body(part, *refs), outs, *args, *sources, *rest
            )
            sources = more or sources
            fulls.append(full)
            passed.append(partner(rounded, "level", 1))
        return fulls, passed

    transfer, smooth = fetched(loads, transfer, smooth)
    residual, iterate = [load_panels], None
    for cycle_index in range(ITERS):
        if cycle_index > 0:
            residual, arrived = in_parts(
                residual_body, (level_table, load_panels), (rounded, *sides), (blocks,)
            )
        current, first = call(
            first_body, (wide, narrow), transfer_table, load_panels, *residual, *arrived,
            transfer, smooth, scratch=[held(block_rows)],
        )
        sides = exchanged(first)
        if cycle_index == 0:
            (blocks,) = fetched(loads, blocks)
        correction, returned = in_parts(
            second_body, (level_table, current, first), (*sides,), (blocks, smooth)
        )
        if cycle_index + 1 < ITERS:
            terms = [] if iterate is None else [iterate]
            iterate, rounded = call(
                update_body, (wide, narrow), transfer_table, *returned, *correction,
                *terms, transfer, scratch=[held(block_rows)],
            )
            sides = exchanged(rounded)
    final = call(
        last_body, jax.ShapeDtypeStruct((load_cols, block_rows * width), jnp.float32),
        transfer_table, *returned, *correction, iterate, transfer, out_specs=HBM,
        scratch=[pltpu.VMEM(wide.shape, jnp.float32), held(block_rows), rowwise],
    )
    return final[None]


def solution(mesh):
    in_specs = (
        P("level", None, "dom"),
        P("level", "dom", None, None, None),
        P("level", "dom", None),
        P("level", "dom", None, None),
        P("level", "dom", None, None, None),
        P("level", "dom", None),
        P("level", "dom", None, None),
    )
    out_specs = P("level", None, "dom")

    return jax.shard_map(local, mesh=mesh, in_specs=in_specs, out_specs=out_specs, check_vma=False)
```

```python
import jax
import jax.numpy as jnp
from jax import lax
from jax.experimental import pallas as pl
from jax.experimental.pallas import tpu as pltpu
from jax.sharding import PartitionSpec as P

ITERS = 2
CHUNK = 4
LIMIT = 16 << 20
LANES = 128
VMEM = pl.BlockSpec(memory_space=pltpu.VMEM)
HBM = pl.BlockSpec(memory_space=pltpu.HBM)
NT = (((1,), (1,)), ((), ()))


def partner(x, axis, apart):
    return lax.ppermute(x, axis, [(i, i ^ 1 << apart) for i in range(lax.axis_size(axis))])


def swapped(x, axis, first):
    size = lax.axis_size(axis)
    pairs = [(i % size, (i + 1) % size) for i in range(first, first + size, 2)]
    return lax.ppermute(x, axis, pairs + [(b, a) for a, b in pairs])


def like(x):
    return jax.ShapeDtypeStruct(x.shape, x.dtype)


def inside(x):
    return pltpu.with_memory_space_constraint(x, pltpu.HBM)


def call(body, outs, *args, in_specs=None, out_specs=None, scratch=(), cost=None):
    if cost is None:
        size = sum(x.size * x.dtype.itemsize for x in (*args, *jax.tree.leaves(outs)))
        cost = pl.CostEstimate(flops=64 * size, bytes_accessed=size, transcendentals=0)
    return pl.pallas_call(
        body,
        out_shape=outs,
        in_specs=in_specs or [VMEM] * len(args),
        out_specs=out_specs or jax.tree.map(lambda _: VMEM, outs),
        scratch_shapes=list(scratch),
        cost_estimate=cost,
        compiler_params=pltpu.CompilerParams(vmem_limit_bytes=LIMIT),
    )(*args)


def entry(table, at):
    return table[at : at + 1, 0:1][0, 0]


def is_fine(table):
    return entry(table, table.shape[0] - 1) == 1


def times(panel, block):
    return lax.dot_general(panel, block, NT, preferred_element_type=jnp.float32)


def gathered(source, table, row, blocks):
    count = blocks.shape[1]
    left = jnp.concatenate([source[entry(table, row * count + k)] for k in range(count)], axis=1)
    right = jnp.concatenate([blocks[row, k] for k in range(count)], axis=1)
    return times(left, right)


def joined(parts, scratch):
    at = 0
    for part in parts:
        for i in range(part.shape[0]):
            scratch[at + i] = part[i]
        at += part.shape[0]


def open_body(loads, panels, sent, arrivals):
    rows, _, width = panels.shape
    copies = [
        pltpu.make_async_copy(
            loads.at[:, pl.ds(i * width, width)], panels.at[i], arrivals.at[i]
        )
        for i in range(rows)
    ]
    for copy in copies:
        copy.start()
    for i, copy in enumerate(copies):
        copy.wait()
        sent[i] = panels[i].astype(jnp.bfloat16)


def pack_body(table, source, *outs):
    for side, out in enumerate(outs):
        for j in range(out.shape[0]):
            out[j] = source[entry(table, side * out.shape[0] + j)]


def first_body(fetch, table, loads, *refs):
    if fetch:
        *refs, arrivals = refs
        *pieces, source, smoother, current, first, transfer, scratch = refs
        copies = [
            pltpu.make_async_copy(source.at[i], transfer.at[i], arrivals.at[i])
            for i in range(source.shape[0])
        ]
    else:
        *pieces, transfer, smoother, current, first, scratch = refs
        copies = []
    for copy in copies:
        copy.start()
    residual, arrived = pieces[: len(pieces) // 2], pieces[len(pieces) // 2 :]
    rows = first.shape[0]

    @pl.when(is_fine(table))
    def _():
        joined(residual, current)
        for copy in copies:
            copy.wait()

    @pl.when(jnp.logical_not(is_fine(table)))
    def _():
        joined(arrived, scratch)
        for i in range(rows):
            if i % CHUNK == 0:
                for copy in copies[i : i + CHUNK]:
                    copy.wait()
            current[i] = loads[i] + gathered(scratch, table, i, transfer)

    for i in range(rows):
        value = times(current[i].astype(jnp.bfloat16), smoother[i])
        first[i] = value.astype(jnp.bfloat16)


def second_rows(low, targets, table, current, first, extension, blocks, smoother, rounded):
    places = [(full, i) for full in targets for i in range(full.shape[0])]
    for at in range(len(places)):
        applied = gathered(extension, table, low + at, blocks)
        rounded[at] = (current[low + at] - applied).astype(jnp.bfloat16)
    for at, (full, i) in enumerate(places):
        value = first[low + at].astype(jnp.float32) + times(rounded[at], smoother[low + at])
        full[i] = value
        if full is targets[0]:
            rounded[at] = value.astype(jnp.bfloat16)


def second_start_body(table, current, first, left, right, sibling, blocks, smoother, full, rounded, extension, rest, scratch):
    joined([first, left, right, sibling], extension)

    @pl.when(is_fine(table))
    def _():
        second_rows(0, (full, rest), table, current, first, extension, blocks, smoother, scratch)

    @pl.when(jnp.logical_not(is_fine(table)))
    def _():
        second_rows(0, (full,), table, current, first, extension, blocks, smoother, rounded)


def second_end_body(table, current, first, extension, blocks, smoother, full, rounded):
    @pl.when(jnp.logical_not(is_fine(table)))
    def _():
        low = first.shape[0] - full.shape[0]
        second_rows(low, (full,), table, current, first, extension, blocks, smoother, rounded)


def row_of(parts, at):
    for part in parts:
        if at < part.shape[0]:
            return part[at]
        at -= part.shape[0]


def update_body(table, early, late, correction, rest, *refs):
    *terms, transfer, iterate, rounded, scratch = refs

    @pl.when(is_fine(table))
    def _():
        joined((early, late), scratch)
        for i in range(iterate.shape[0]):
            value = row_of((correction, rest), i)
            for term in terms:
                value = term[i] + value
            value = value + gathered(scratch, table, i, transfer)
            iterate[i] = value
            rounded[i] = value.astype(jnp.bfloat16)


def residual_body(low, table, loads, *refs):
    *sources, blocks, residual, sent = refs[: len(refs) - (low == 0)]

    @pl.when(is_fine(table))
    def _():
        if low == 0:
            extension = refs[-1]
            joined(sources, extension)
        else:
            (extension,) = sources
        for i in range(residual.shape[0]):
            value = loads[low + i] - gathered(extension, table, low + i, blocks)
            residual[i] = value
            sent[i] = value.astype(jnp.bfloat16)


def last_body(table, early, late, correction, rest, end, iterate, transfer, out, total, scratch, leaves):
    rows, _, width = total.shape
    copies = [
        pltpu.make_async_copy(total.at[i], out.at[:, pl.ds(i * width, width)], leaves.at[i])
        for i in range(rows)
    ]

    @pl.when(is_fine(table))
    def _():
        joined((early, late), scratch)
        for i in range(rows):
            value = iterate[i] + row_of((correction, rest), i)
            total[i] = value + gathered(scratch, table, i, transfer)
            copies[i].start()

    @pl.when(jnp.logical_not(is_fine(table)))
    def _():
        for i in range(rows):
            total[i] = row_of((correction, end), i)
            copies[i].start()

    for copy in copies:
        copy.wait()


def local(loads, level_blocks, level_cols, smoother, transfer_blocks, transfer_cols, bound_rows):
    block_rows = level_cols.shape[1]
    width = level_blocks.shape[-1]
    load_cols = loads.shape[1]
    list_width = bound_rows.shape[-1]
    left_list, right_list, sibling_list = bound_rows[0, 0]
    blocks, smooth, transfer, loads = level_blocks[0], smoother[0], transfer_blocks[0], loads[0]

    def panels(count, kind):
        return jax.ShapeDtypeStruct((count, load_cols, width), kind)

    def held(count):
        return pltpu.VMEM((count, load_cols, width), jnp.bfloat16)

    wide, narrow = panels(block_rows, jnp.float32), panels(block_rows, jnp.bfloat16)
    early_rows = block_rows // 4
    late_rows = block_rows - early_rows
    listed = panels(list_width, jnp.bfloat16)
    extended = panels(block_rows + 3 * list_width, jnp.bfloat16)
    rowwise = pltpu.SemaphoreType.DMA((block_rows,))

    load_panels, sent = call(
        open_body, (wide, narrow), inside(loads), in_specs=[HBM], scratch=[rowwise],
        cost=pl.CostEstimate(flops=5_000_000_000, bytes_accessed=2 * loads.size * 4, transcendentals=0),
    )
    arrived = [partner(sent, "level", 1)]

    even = lax.axis_index("dom") % 2 == 0
    ahead = swapped(jnp.where(even, right_list, left_list), "dom", 0)
    behind = swapped(jnp.where(even, left_list, right_list), "dom", 1)
    wanted = jnp.concatenate([ahead, behind, partner(sibling_list, "level", 0)])
    columns = level_cols.reshape(-1)
    from_left = (columns >= block_rows) & (columns < block_rows + list_width)
    from_right = (columns >= block_rows + list_width) & (columns < block_rows + 2 * list_width)
    moved = jnp.where(from_left, list_width, 0) - jnp.where(from_right, list_width, 0)
    columns = columns + jnp.where(even, moved, 0)
    fine = (lax.axis_index("level") < 2).astype(jnp.int32).reshape(1)

    def spread(values):
        return jnp.broadcast_to(values[:, None], (values.shape[0], LANES))

    level_table = spread(jnp.concatenate([columns, fine]))
    transfer_table = spread(jnp.concatenate([transfer_cols.reshape(-1), fine]))
    wanted_table = spread(wanted)

    def exchanged(source):
        ahead, behind, beside = call(pack_body, (listed,) * 3, wanted_table, source)
        ahead = swapped(ahead, "dom", 0)
        behind = swapped(behind, "dom", 1)
        return ahead, behind, partner(beside, "level", 0)

    def part(rows):
        return panels(rows, jnp.float32), panels(rows, jnp.bfloat16)

    def sent_on(x):
        return partner(x, "level", 1)

    residual, iterate = [load_panels], None
    for cycle_index in range(ITERS):
        if cycle_index > 0:
            args = (level_table, load_panels)
            early, sent, extension = call(
                lambda *refs: residual_body(0, *refs), part(early_rows) + (extended,),
                *args, rounded, *sides, blocks,
            )
            arrived = [sent_on(sent)]
            late, sent = call(
                lambda *refs: residual_body(early_rows, *refs), part(late_rows),
                *args, extension, blocks,
            )
            arrived.append(partner(sent, "level", 1))
            residual = [early, late]
        fetch = cycle_index == 0
        current, first, *kept = call(
            lambda *refs: first_body(fetch, *refs), (wide, narrow) + (like(transfer),) * fetch,
            transfer_table, load_panels, *residual, *arrived,
            inside(transfer) if fetch else transfer, smooth,
            in_specs=[VMEM] * (2 + len(residual) + len(arrived)) + [HBM if fetch else VMEM, VMEM],
            scratch=[held(block_rows)] + [rowwise] * fetch,
        )
        (transfer,) = kept or (transfer,)
        sides = exchanged(first)
        args = (level_table, current, first)
        correction, rounded, extension, rest = call(
            second_start_body,
            part(early_rows) + (extended, panels(late_rows, jnp.float32)),
            *args, *sides, blocks, smooth, scratch=[held(block_rows)],
        )
        returned = [sent_on(rounded)]
        end, rounded = call(second_end_body, part(late_rows), *args, extension, blocks, smooth)
        returned.append(partner(rounded, "level", 1))
        if cycle_index + 1 < ITERS:
            terms = [] if iterate is None else [iterate]
            iterate, rounded = call(
                update_body, (wide, narrow), transfer_table, *returned, correction, rest,
                *terms, transfer, scratch=[held(block_rows)],
            )
            sides = exchanged(rounded)
    final = call(
        last_body, jax.ShapeDtypeStruct((load_cols, block_rows * width), jnp.float32),
        transfer_table, *returned, correction, rest, end, iterate, transfer, out_specs=HBM,
        scratch=[pltpu.VMEM(wide.shape, jnp.float32), held(block_rows), rowwise],
    )
    return final[None]


def solution(mesh):
    in_specs = (
        P("level", None, "dom"),
        P("level", "dom", None, None, None),
        P("level", "dom", None),
        P("level", "dom", None, None),
        P("level", "dom", None, None, None),
        P("level", "dom", None),
        P("level", "dom", None, None),
    )
    out_specs = P("level", None, "dom")

    return jax.shard_map(local, mesh=mesh, in_specs=in_specs, out_specs=out_specs, check_vma=False)
```

```python
import jax
import jax.numpy as jnp
from jax import lax
from jax.experimental import pallas as pl
from jax.experimental.pallas import tpu as pltpu
from jax.sharding import PartitionSpec as P

ITERS = 2
LIMIT = 16 << 20
LANES = 128
VMEM = pl.BlockSpec(memory_space=pltpu.VMEM)
HBM = pl.BlockSpec(memory_space=pltpu.HBM)
NT = (((1,), (1,)), ((), ()))


def partner(x, axis, apart):
    return lax.ppermute(x, axis, [(i, i ^ 1 << apart) for i in range(lax.axis_size(axis))])


def swapped(x, axis, first):
    size = lax.axis_size(axis)
    pairs = [(i % size, (i + 1) % size) for i in range(first, first + size, 2)]
    return lax.ppermute(x, axis, pairs + [(b, a) for a, b in pairs])


def like(x):
    return jax.ShapeDtypeStruct(x.shape, x.dtype)


def inside(x):
    return pltpu.with_memory_space_constraint(x, pltpu.HBM)


def call(body, outs, *args, in_specs=None, out_specs=None, scratch=(), cost=None):
    if cost is None:
        size = sum(x.size * x.dtype.itemsize for x in (*args, *jax.tree.leaves(outs)))
        cost = pl.CostEstimate(flops=64 * size, bytes_accessed=size, transcendentals=0)
    return pl.pallas_call(
        body,
        out_shape=outs,
        in_specs=in_specs or [VMEM] * len(args),
        out_specs=out_specs or jax.tree.map(lambda _: VMEM, outs),
        scratch_shapes=list(scratch),
        cost_estimate=cost,
        compiler_params=pltpu.CompilerParams(vmem_limit_bytes=LIMIT),
    )(*args)


def entry(table, at):
    return table[at : at + 1, 0:1][0, 0]


def is_fine(table):
    return entry(table, table.shape[0] - 1) == 1


def times(panel, block):
    return lax.dot_general(panel, block, NT, preferred_element_type=jnp.float32)


def gathered(source, table, row, blocks):
    count = blocks.shape[1]
    left = jnp.concatenate([source[entry(table, row * count + k)] for k in range(count)], axis=1)
    right = jnp.concatenate([blocks[row, k] for k in range(count)], axis=1)
    return times(left, right)


def joined(parts, scratch):
    at = 0
    for part in parts:
        for i in range(part.shape[0]):
            scratch[at + i] = part[i]
        at += part.shape[0]


def open_body(loads, panels, sent, arrivals):
    rows, _, width = panels.shape
    copies = [
        pltpu.make_async_copy(
            loads.at[:, pl.ds(i * width, width)], panels.at[i], arrivals.at[i]
        )
        for i in range(rows)
    ]
    for copy in copies:
        copy.start()
    for i, copy in enumerate(copies):
        copy.wait()
        sent[i] = panels[i].astype(jnp.bfloat16)


def pack_body(table, source, *outs):
    for side, out in enumerate(outs):
        for j in range(out.shape[0]):
            out[j] = source[entry(table, side * out.shape[0] + j)]


def fetch_body(_, source, target, arrivals):
    copies = [
        pltpu.make_async_copy(source.at[i], target.at[i], arrivals.at[i])
        for i in range(source.shape[0])
    ]
    for copy in copies:
        copy.start()
    for copy in copies:
        copy.wait()


def first_body(table, loads, *refs):
    *pieces, transfer, smoother, current, first, scratch = refs
    residual, arrived = pieces[: len(pieces) // 2], pieces[len(pieces) // 2 :]
    rows = first.shape[0]

    @pl.when(is_fine(table))
    def _():
        joined(residual, current)

    @pl.when(jnp.logical_not(is_fine(table)))
    def _():
        joined(arrived, scratch)
        for i in range(rows):
            current[i] = loads[i] + gathered(scratch, table, i, transfer)

    for i in range(rows):
        value = times(current[i].astype(jnp.bfloat16), smoother[i])
        first[i] = value.astype(jnp.bfloat16)


def second_rows(low, table, current, first, extension, blocks, smoother, full, rounded):
    rows = full.shape[0]
    for i in range(rows):
        applied = gathered(extension, table, low + i, blocks)
        rounded[i] = (current[low + i] - applied).astype(jnp.bfloat16)
    for i in range(rows):
        value = first[low + i].astype(jnp.float32) + times(rounded[i], smoother[low + i])
        full[i] = value
        rounded[i] = value.astype(jnp.bfloat16)


def second_start_body(table, current, first, left, right, sibling, blocks, smoother, full, rounded, extension):
    joined([first, left, right, sibling], extension)

    @pl.when(jnp.logical_not(is_fine(table)))
    def _():
        second_rows(0, table, current, first, extension, blocks, smoother, full, rounded)


def second_end_body(table, current, first, extension, blocks, smoother, full, rounded):
    @pl.when(jnp.logical_not(is_fine(table)))
    def _():
        low = first.shape[0] - full.shape[0]
        second_rows(low, table, current, first, extension, blocks, smoother, full, rounded)


def second_fine_body(table, current, first, extension, blocks, smoother, full, scratch):
    @pl.when(is_fine(table))
    def _():
        second_rows(0, table, current, first, extension, blocks, smoother, full, scratch)


def row_of(parts, at):
    for part in parts:
        if at < part.shape[0]:
            return part[at]
        at -= part.shape[0]


def update_body(table, early, late, correction, *refs):
    *terms, transfer, iterate, rounded, scratch = refs

    @pl.when(is_fine(table))
    def _():
        joined((early, late), scratch)
        for i in range(iterate.shape[0]):
            value = correction[i]
            for term in terms:
                value = term[i] + value
            value = value + gathered(scratch, table, i, transfer)
            iterate[i] = value
            rounded[i] = value.astype(jnp.bfloat16)


def residual_body(low, table, loads, *refs):
    *sources, blocks, residual, sent = refs[: len(refs) - (low == 0)]

    @pl.when(is_fine(table))
    def _():
        if low == 0:
            extension = refs[-1]
            joined(sources, extension)
        else:
            (extension,) = sources
        for i in range(residual.shape[0]):
            value = loads[low + i] - gathered(extension, table, low + i, blocks)
            residual[i] = value
            sent[i] = value.astype(jnp.bfloat16)


def last_body(table, early, late, correction, start, end, iterate, transfer, out, total, scratch, leaves):
    rows, _, width = total.shape
    copies = [
        pltpu.make_async_copy(total.at[i], out.at[:, pl.ds(i * width, width)], leaves.at[i])
        for i in range(rows)
    ]

    @pl.when(is_fine(table))
    def _():
        joined((early, late), scratch)
        for i in range(rows):
            value = iterate[i] + correction[i]
            total[i] = value + gathered(scratch, table, i, transfer)
            copies[i].start()

    @pl.when(jnp.logical_not(is_fine(table)))
    def _():
        for i in range(rows):
            total[i] = row_of((start, end), i)
            copies[i].start()

    for copy in copies:
        copy.wait()


def local(loads, level_blocks, level_cols, smoother, transfer_blocks, transfer_cols, bound_rows):
    block_rows = level_cols.shape[1]
    width = level_blocks.shape[-1]
    load_cols = loads.shape[1]
    list_width = bound_rows.shape[-1]
    left_list, right_list, sibling_list = bound_rows[0, 0]
    blocks, smooth, transfer, loads = level_blocks[0], smoother[0], transfer_blocks[0], loads[0]

    def panels(count, kind):
        return jax.ShapeDtypeStruct((count, load_cols, width), kind)

    def held(count):
        return pltpu.VMEM((count, load_cols, width), jnp.bfloat16)

    wide, narrow = panels(block_rows, jnp.float32), panels(block_rows, jnp.bfloat16)
    early_rows = block_rows * 3 // 8
    late_rows = block_rows - early_rows
    listed = panels(list_width, jnp.bfloat16)
    extended = panels(block_rows + 3 * list_width, jnp.bfloat16)
    rowwise = pltpu.SemaphoreType.DMA((block_rows,))

    load_panels, sent = call(
        open_body, (wide, narrow), inside(loads), in_specs=[HBM], scratch=[rowwise],
        cost=pl.CostEstimate(flops=5_000_000_000, bytes_accessed=2 * loads.size * 4, transcendentals=0),
    )
    arrived = [partner(sent, "level", 1)]

    even = lax.axis_index("dom") % 2 == 0
    ahead = swapped(jnp.where(even, right_list, left_list), "dom", 0)
    behind = swapped(jnp.where(even, left_list, right_list), "dom", 1)
    wanted = jnp.concatenate([ahead, behind, partner(sibling_list, "level", 0)])
    columns = level_cols.reshape(-1)
    from_left = (columns >= block_rows) & (columns < block_rows + list_width)
    from_right = (columns >= block_rows + list_width) & (columns < block_rows + 2 * list_width)
    moved = jnp.where(from_left, list_width, 0) - jnp.where(from_right, list_width, 0)
    columns = columns + jnp.where(even, moved, 0)
    fine = (lax.axis_index("level") < 2).astype(jnp.int32).reshape(1)

    def spread(values):
        return jnp.broadcast_to(values[:, None], (values.shape[0], LANES))

    level_table = spread(jnp.concatenate([columns, fine]))
    transfer_table = spread(jnp.concatenate([transfer_cols.reshape(-1), fine]))
    wanted_table = spread(wanted)

    def fetched(source):
        return call(fetch_body, like(source), inside(loads), inside(source), in_specs=[HBM, HBM], scratch=[rowwise])

    def exchanged(source):
        ahead, behind, beside = call(pack_body, (listed,) * 3, wanted_table, source)
        ahead = swapped(ahead, "dom", 0)
        behind = swapped(behind, "dom", 1)
        beside = partner(beside, "level", 0)
        return ahead, behind, beside

    def part(rows):
        return panels(rows, jnp.float32), panels(rows, jnp.bfloat16)

    def sent_on(x):
        return partner(x, "level", 1)

    transfer = fetched(transfer)
    residual, iterate = [load_panels], None
    for cycle_index in range(ITERS):
        if cycle_index > 0:
            args = (level_table, load_panels)
            early, sent, extension = call(
                lambda *refs: residual_body(0, *refs), part(early_rows) + (extended,),
                *args, rounded, *sides, blocks,
            )
            arrived = [sent_on(sent)]
            late, sent = call(
                lambda *refs: residual_body(early_rows, *refs), part(late_rows),
                *args, extension, blocks,
            )
            arrived.append(partner(sent, "level", 1))
            residual = [early, late]
        current, first = call(
            first_body, (wide, narrow), transfer_table, load_panels, *residual, *arrived,
            transfer, smooth, scratch=[held(block_rows)],
        )
        sides = exchanged(first)
        if cycle_index == 0:
            blocks = fetched(blocks)
        args = (level_table, current, first)
        start, rounded, extension = call(
            second_start_body, part(early_rows) + (extended,), *args, *sides, blocks, smooth
        )
        returned = [sent_on(rounded)]
        end, rounded = call(second_end_body, part(late_rows), *args, extension, blocks, smooth)
        returned.append(sent_on(rounded))
        correction = call(second_fine_body, wide, *args, extension, blocks, smooth, scratch=[held(block_rows)])
        if cycle_index + 1 < ITERS:
            terms = [] if iterate is None else [iterate]
            iterate, rounded = call(
                update_body, (wide, narrow), transfer_table, *returned, correction,
                *terms, transfer, scratch=[held(block_rows)],
            )
            sides = exchanged(rounded)
    final = call(
        last_body, jax.ShapeDtypeStruct((load_cols, block_rows * width), jnp.float32),
        transfer_table, *returned, correction, start, end, iterate, transfer, out_specs=HBM,
        scratch=[pltpu.VMEM(wide.shape, jnp.float32), held(block_rows), rowwise],
    )
    return final[None]


def solution(mesh):
    in_specs = (
        P("level", None, "dom"),
        P("level", "dom", None, None, None),
        P("level", "dom", None),
        P("level", "dom", None, None),
        P("level", "dom", None, None, None),
        P("level", "dom", None),
        P("level", "dom", None, None),
    )
    out_specs = P("level", None, "dom")

    return jax.shard_map(local, mesh=mesh, in_specs=in_specs, out_specs=out_specs, check_vma=False)
```

```python
import jax
import jax.numpy as jnp
from jax import lax
from jax.experimental import pallas as pl
from jax.experimental.pallas import tpu as pltpu
from jax.sharding import PartitionSpec as P

ITERS = 2
LIMIT = 16 << 20
LANES = 128
VMEM = pl.BlockSpec(memory_space=pltpu.VMEM)
HBM = pl.BlockSpec(memory_space=pltpu.HBM)
NT = (((1,), (1,)), ((), ()))


def partner(x, axis, apart):
    return lax.ppermute(x, axis, [(i, i ^ 1 << apart) for i in range(lax.axis_size(axis))])


def swapped(x, axis, first):
    size = lax.axis_size(axis)
    pairs = [(i % size, (i + 1) % size) for i in range(first, first + size, 2)]
    return lax.ppermute(x, axis, pairs + [(b, a) for a, b in pairs])


def like(x):
    return jax.ShapeDtypeStruct(x.shape, x.dtype)


def inside(x):
    return pltpu.with_memory_space_constraint(x, pltpu.HBM)


def call(body, outs, *args, in_specs=None, out_specs=None, scratch=(), cost=None):
    if cost is None:
        size = sum(x.size * x.dtype.itemsize for x in (*args, *jax.tree.leaves(outs)))
        cost = pl.CostEstimate(flops=64 * size, bytes_accessed=size, transcendentals=0)
    return pl.pallas_call(
        body,
        out_shape=outs,
        in_specs=in_specs or [VMEM] * len(args),
        out_specs=out_specs or jax.tree.map(lambda _: VMEM, outs),
        scratch_shapes=list(scratch),
        cost_estimate=cost,
        compiler_params=pltpu.CompilerParams(vmem_limit_bytes=LIMIT),
    )(*args)


def entry(table, at):
    return table[at : at + 1, 0:1][0, 0]


def is_fine(table):
    return entry(table, table.shape[0] - 1) == 1


def times(panel, block):
    return lax.dot_general(panel, block, NT, preferred_element_type=jnp.float32)


def gathered(source, table, row, blocks):
    count = blocks.shape[1]
    left = jnp.concatenate([source[entry(table, row * count + k)] for k in range(count)], axis=1)
    right = jnp.concatenate([blocks[row, k] for k in range(count)], axis=1)
    return times(left, right)


def joined(parts, scratch):
    at = 0
    for part in parts:
        for i in range(part.shape[0]):
            scratch[at + i] = part[i]
        at += part.shape[0]


def open_body(loads, panels, sent, arrivals):
    rows, _, width = panels.shape
    copies = [
        pltpu.make_async_copy(
            loads.at[:, pl.ds(i * width, width)], panels.at[i], arrivals.at[i]
        )
        for i in range(rows)
    ]
    for copy in copies:
        copy.start()
    for i, copy in enumerate(copies):
        copy.wait()
        sent[i] = panels[i].astype(jnp.bfloat16)


def pack_body(table, source, *outs):
    for side, out in enumerate(outs):
        for j in range(out.shape[0]):
            out[j] = source[entry(table, side * out.shape[0] + j)]


def fetch_body(_, source, target, arrivals):
    copies = [
        pltpu.make_async_copy(source.at[i], target.at[i], arrivals.at[i])
        for i in range(source.shape[0])
    ]
    for copy in copies:
        copy.start()
    for copy in copies:
        copy.wait()


def first_body(table, loads, *refs):
    *pieces, transfer, smoother, current, first, scratch = refs
    residual, arrived = pieces[: len(pieces) // 2], pieces[len(pieces) // 2 :]
    rows = first.shape[0]

    @pl.when(is_fine(table))
    def _():
        joined(residual, current)

    @pl.when(jnp.logical_not(is_fine(table)))
    def _():
        joined(arrived, scratch)
        for i in range(rows):
            current[i] = loads[i] + gathered(scratch, table, i, transfer)

    for i in range(rows):
        value = times(current[i].astype(jnp.bfloat16), smoother[i])
        first[i] = value.astype(jnp.bfloat16)


def second_rows(low, table, current, first, extension, blocks, smoother, rounded, full=None):
    rows = rounded.shape[0]
    for i in range(rows):
        applied = gathered(extension, table, low + i, blocks)
        rounded[i] = (current[low + i] - applied).astype(jnp.bfloat16)
    for i in range(rows):
        value = first[low + i].astype(jnp.float32) + times(rounded[i], smoother[low + i])
        rounded[i] = value.astype(jnp.bfloat16)
        if full is not None:
            full[i] = value


def second_start_body(table, current, first, left, right, sibling, blocks, smoother, rounded, extension, *full):
    joined([first, left, right, sibling], extension)

    @pl.when(jnp.logical_not(is_fine(table)))
    def _():
        second_rows(0, table, current, first, extension, blocks, smoother, rounded, *full)


def second_end_body(table, current, first, extension, blocks, smoother, rounded, *full):
    @pl.when(jnp.logical_not(is_fine(table)))
    def _():
        low = first.shape[0] - rounded.shape[0]
        second_rows(low, table, current, first, extension, blocks, smoother, rounded, *full)


def second_fine_body(table, current, first, extension, blocks, smoother, full, scratch):
    @pl.when(is_fine(table))
    def _():
        second_rows(0, table, current, first, extension, blocks, smoother, scratch, full)


def row_of(parts, at):
    for part in parts:
        if at < part.shape[0]:
            return part[at]
        at -= part.shape[0]


def update_body(table, early, late, correction, *refs):
    *terms, transfer, iterate, rounded, scratch = refs

    @pl.when(is_fine(table))
    def _():
        joined((early, late), scratch)
        for i in range(iterate.shape[0]):
            value = correction[i]
            for term in terms:
                value = term[i] + value
            value = value + gathered(scratch, table, i, transfer)
            iterate[i] = value
            rounded[i] = value.astype(jnp.bfloat16)


def residual_body(low, table, loads, *refs):
    *sources, blocks, residual, sent = refs[: len(refs) - (low == 0)]

    @pl.when(is_fine(table))
    def _():
        if low == 0:
            extension = refs[-1]
            joined(sources, extension)
        else:
            (extension,) = sources
        for i in range(residual.shape[0]):
            value = loads[low + i] - gathered(extension, table, low + i, blocks)
            residual[i] = value
            sent[i] = value.astype(jnp.bfloat16)


def last_body(table, early, late, correction, start, end, iterate, transfer, out, total, scratch, leaves):
    rows, _, width = total.shape
    copies = [
        pltpu.make_async_copy(total.at[i], out.at[:, pl.ds(i * width, width)], leaves.at[i])
        for i in range(rows)
    ]

    @pl.when(is_fine(table))
    def _():
        joined((early, late), scratch)
        for i in range(rows):
            value = iterate[i] + correction[i]
            total[i] = value + gathered(scratch, table, i, transfer)
            copies[i].start()

    @pl.when(jnp.logical_not(is_fine(table)))
    def _():
        for i in range(rows):
            total[i] = row_of((start, end), i)
            copies[i].start()

    for copy in copies:
        copy.wait()


def local(loads, level_blocks, level_cols, smoother, transfer_blocks, transfer_cols, bound_rows):
    block_rows = level_cols.shape[1]
    width = level_blocks.shape[-1]
    load_cols = loads.shape[1]
    list_width = bound_rows.shape[-1]
    left_list, right_list, sibling_list = bound_rows[0, 0]
    blocks, smooth, transfer, loads = level_blocks[0], smoother[0], transfer_blocks[0], loads[0]

    def panels(count, kind):
        return jax.ShapeDtypeStruct((count, load_cols, width), kind)

    def held(count):
        return pltpu.VMEM((count, load_cols, width), jnp.bfloat16)

    wide, narrow = panels(block_rows, jnp.float32), panels(block_rows, jnp.bfloat16)
    early_rows = block_rows * 3 // 8
    late_rows = block_rows - early_rows
    listed = panels(list_width, jnp.bfloat16)
    extended = panels(block_rows + 3 * list_width, jnp.bfloat16)
    rowwise = pltpu.SemaphoreType.DMA((block_rows,))

    load_panels, sent = call(
        open_body, (wide, narrow), inside(loads), in_specs=[HBM], scratch=[rowwise],
        cost=pl.CostEstimate(flops=5_000_000_000, bytes_accessed=2 * loads.size * 4, transcendentals=0),
    )
    arrived = [partner(sent, "level", 1)]

    even = lax.axis_index("dom") % 2 == 0
    ahead = swapped(jnp.where(even, right_list, left_list), "dom", 0)
    behind = swapped(jnp.where(even, left_list, right_list), "dom", 1)
    wanted = jnp.concatenate([ahead, behind, partner(sibling_list, "level", 0)])
    columns = level_cols.reshape(-1)
    from_left = (columns >= block_rows) & (columns < block_rows + list_width)
    from_right = (columns >= block_rows + list_width) & (columns < block_rows + 2 * list_width)
    moved = jnp.where(from_left, list_width, 0) - jnp.where(from_right, list_width, 0)
    columns = columns + jnp.where(even, moved, 0)
    fine = (lax.axis_index("level") < 2).astype(jnp.int32).reshape(1)

    def spread(values):
        return jnp.broadcast_to(values[:, None], (values.shape[0], LANES))

    level_table = spread(jnp.concatenate([columns, fine]))
    transfer_table = spread(jnp.concatenate([transfer_cols.reshape(-1), fine]))
    wanted_table = spread(wanted)

    def fetched(source):
        return call(fetch_body, like(source), inside(loads), inside(source), in_specs=[HBM, HBM], scratch=[rowwise])

    def exchanged(source):
        ahead, behind, beside = call(pack_body, (listed,) * 3, wanted_table, source)
        ahead = swapped(ahead, "dom", 0)
        behind = swapped(behind, "dom", 1)
        beside = partner(beside, "level", 0)
        return ahead, behind, beside

    def part(rows):
        return panels(rows, jnp.float32), panels(rows, jnp.bfloat16)

    def sent_on(x):
        return partner(x, "level", 1)

    transfer = fetched(transfer)
    residual, iterate = [load_panels], None
    for cycle_index in range(ITERS):
        if cycle_index > 0:
            args = (level_table, load_panels)
            early, sent, extension = call(
                lambda *refs: residual_body(0, *refs), part(early_rows) + (extended,),
                *args, rounded, *sides, blocks,
            )
            arrived = [sent_on(sent)]
            late, sent = call(
                lambda *refs: residual_body(early_rows, *refs), part(late_rows),
                *args, extension, blocks,
            )
            arrived.append(partner(sent, "level", 1))
            residual = [early, late]
        current, first = call(
            first_body, (wide, narrow), transfer_table, load_panels, *residual, *arrived,
            transfer, smooth, scratch=[held(block_rows)],
        )
        sides = exchanged(first)
        if cycle_index == 0:
            blocks = fetched(blocks)
        args = (level_table, current, first)
        ends = cycle_index + 1 == ITERS
        rounded, extension, *start = call(
            second_start_body,
            (panels(early_rows, jnp.bfloat16), extended) + (panels(early_rows, jnp.float32),) * ends,
            *args, *sides, blocks, smooth,
        )
        returned = [sent_on(rounded)]
        rounded, *end = call(
            second_end_body,
            (panels(late_rows, jnp.bfloat16),) + (panels(late_rows, jnp.float32),) * ends,
            *args, extension, blocks, smooth,
        )
        returned.append(sent_on(rounded))
        correction = call(second_fine_body, wide, *args, extension, blocks, smooth, scratch=[held(block_rows)])
        if not ends:
            terms = [] if iterate is None else [iterate]
            iterate, rounded = call(
                update_body, (wide, narrow), transfer_table, *returned, correction,
                *terms, transfer, scratch=[held(block_rows)],
            )
            sides = exchanged(rounded)
    final = call(
        last_body, jax.ShapeDtypeStruct((load_cols, block_rows * width), jnp.float32),
        transfer_table, *returned, correction, *start, *end, iterate, transfer, out_specs=HBM,
        scratch=[pltpu.VMEM(wide.shape, jnp.float32), held(block_rows), rowwise],
    )
    return final[None]


def solution(mesh):
    in_specs = (
        P("level", None, "dom"),
        P("level", "dom", None, None, None),
        P("level", "dom", None),
        P("level", "dom", None, None),
        P("level", "dom", None, None, None),
        P("level", "dom", None),
        P("level", "dom", None, None),
    )
    out_specs = P("level", None, "dom")

    return jax.shard_map(local, mesh=mesh, in_specs=in_specs, out_specs=out_specs, check_vma=False)
```

```python
import jax
import jax.numpy as jnp
from jax import lax
from jax.experimental import pallas as pl
from jax.experimental.pallas import tpu as pltpu
from jax.sharding import PartitionSpec as P

ITERS = 2
LIMIT = 16 << 20
LANES = 128
VMEM = pl.BlockSpec(memory_space=pltpu.VMEM)
HBM = pl.BlockSpec(memory_space=pltpu.HBM)
NT = (((1,), (1,)), ((), ()))


def partner(x, axis, apart):
    return lax.ppermute(x, axis, [(i, i ^ 1 << apart) for i in range(lax.axis_size(axis))])


def swapped(x, axis, first):
    size = lax.axis_size(axis)
    pairs = [(i % size, (i + 1) % size) for i in range(first, first + size, 2)]
    return lax.ppermute(x, axis, pairs + [(b, a) for a, b in pairs])


def like(x):
    return jax.ShapeDtypeStruct(x.shape, x.dtype)


def inside(x):
    return pltpu.with_memory_space_constraint(x, pltpu.HBM)


def call(body, outs, *args, in_specs=None, out_specs=None, scratch=(), cost=None):
    if cost is None:
        size = sum(x.size * x.dtype.itemsize for x in (*args, *jax.tree.leaves(outs)))
        cost = pl.CostEstimate(flops=64 * size, bytes_accessed=size, transcendentals=0)
    return pl.pallas_call(
        body,
        out_shape=outs,
        in_specs=in_specs or [VMEM] * len(args),
        out_specs=out_specs or jax.tree.map(lambda _: VMEM, outs),
        scratch_shapes=list(scratch),
        cost_estimate=cost,
        compiler_params=pltpu.CompilerParams(vmem_limit_bytes=LIMIT),
    )(*args)


def entry(table, at):
    return table[pl.ds(at, 1), 0:1][0, 0]


def is_fine(table):
    return entry(table, table.shape[0] - 1) == 1


def times(panel, block):
    return lax.dot_general(panel, block, NT, preferred_element_type=jnp.float32)


def gathered(source, table, row, blocks):
    count = blocks.shape[1]
    left = jnp.concatenate([source[entry(table, row * count + k)] for k in range(count)], axis=1)
    right = jnp.concatenate([blocks[row, k] for k in range(count)], axis=1)
    return times(left, right)


def joined(parts, scratch):
    at = 0
    for part in parts:
        for i in range(part.shape[0]):
            scratch[at + i] = part[i]
        at += part.shape[0]


def open_body(loads, panels, sent, arrivals):
    rows, _, width = panels.shape
    copies = [
        pltpu.make_async_copy(
            loads.at[:, pl.ds(i * width, width)], panels.at[i], arrivals.at[i]
        )
        for i in range(rows)
    ]
    for copy in copies:
        copy.start()
    for i, copy in enumerate(copies):
        copy.wait()
        sent[i] = panels[i].astype(jnp.bfloat16)


def fetch_body(_, source, target, arrivals):
    copies = [
        pltpu.make_async_copy(source.at[i], target.at[i], arrivals.at[i])
        for i in range(source.shape[0])
    ]
    for copy in copies:
        copy.start()
    for copy in copies:
        copy.wait()


def chosen(wanted, outs):
    return [(entry(rows, j), out, j) for rows, out in zip(wanted, outs) for j in range(out.shape[0])]


def first_listed_body(lists, pieces, table, loads, *refs):
    wanted, refs = refs[:lists], refs[lists:]
    residual, arrived, refs = refs[:pieces], refs[pieces : 2 * pieces], refs[2 * pieces :]
    transfer, smoother, *refs, scratch = refs
    outs = refs[:lists]
    places = chosen(wanted, outs)
    if pieces > 1:
        joined_residual, joined_arrived = refs[lists:]
    else:
        (joined_residual,), (joined_arrived,) = residual, arrived

    @pl.when(is_fine(table))
    def _():
        if pieces > 1:
            joined(residual, joined_residual)
        for at, (row, _, _) in enumerate(places):
            scratch[at] = joined_residual[row].astype(jnp.bfloat16)

    @pl.when(jnp.logical_not(is_fine(table)))
    def _():
        if pieces > 1:
            joined(arrived, joined_arrived)
        for at, (row, _, _) in enumerate(places):
            value = loads[row] + gathered(joined_arrived, table, row, transfer)
            scratch[at] = value.astype(jnp.bfloat16)

    for at, (row, out, j) in enumerate(places):
        out[j] = times(scratch[at], smoother[row]).astype(jnp.bfloat16)


def first_body(table, loads, residual, arrived, transfer, smoother, current, first):
    rows = first.shape[0]

    @pl.when(is_fine(table))
    def _():
        joined([residual], current)

    @pl.when(jnp.logical_not(is_fine(table)))
    def _():
        for i in range(rows):
            current[i] = loads[i] + gathered(arrived, table, i, transfer)

    for i in range(rows):
        value = times(current[i].astype(jnp.bfloat16), smoother[i])
        first[i] = value.astype(jnp.bfloat16)


def second_rows(low, table, current, first, extension, blocks, smoother, rounded, full=None):
    rows = rounded.shape[0]
    for i in range(rows):
        applied = gathered(extension, table, low + i, blocks)
        rounded[i] = (current[low + i] - applied).astype(jnp.bfloat16)
    for i in range(rows):
        value = first[low + i].astype(jnp.float32) + times(rounded[i], smoother[low + i])
        rounded[i] = value.astype(jnp.bfloat16)
        if full is not None:
            full[i] = value


def second_start_body(table, current, first, left, right, sibling, blocks, smoother, rounded, extension, *full):
    joined([first, left, right, sibling], extension)

    @pl.when(jnp.logical_not(is_fine(table)))
    def _():
        second_rows(0, table, current, first, extension, blocks, smoother, rounded, *full)


def second_end_body(table, current, first, extension, blocks, smoother, rounded, *full):
    @pl.when(jnp.logical_not(is_fine(table)))
    def _():
        low = first.shape[0] - rounded.shape[0]
        second_rows(low, table, current, first, extension, blocks, smoother, rounded, *full)


def second_fine_body(table, current, first, extension, blocks, smoother, full, scratch):
    @pl.when(is_fine(table))
    def _():
        second_rows(0, table, current, first, extension, blocks, smoother, scratch, full)


def row_of(parts, at):
    for part in parts:
        if at < part.shape[0]:
            return part[at]
        at -= part.shape[0]


def updated(row, arrived, table, transfer, correction, terms):
    value = correction[row]
    for term in terms:
        value = term[row] + value
    return value + gathered(arrived, table, row, transfer)


def update_listed_body(lists, pieces, table, *refs):
    wanted, arrived, refs = refs[:lists], refs[lists : lists + pieces], refs[lists + pieces :]
    more = lists + (pieces > 1)
    correction, *terms, transfer = refs[:-more]
    outs = refs[-more:][:lists]

    @pl.when(is_fine(table))
    def _():
        if pieces > 1:
            joined(arrived, refs[-1])
        source = refs[-1] if pieces > 1 else arrived[0]
        for row, out, j in chosen(wanted, outs):
            value = updated(row, source, table, transfer, correction, terms)
            out[j] = value.astype(jnp.bfloat16)


def update_body(table, arrived, correction, *refs):
    *terms, transfer, iterate, rounded = refs

    @pl.when(is_fine(table))
    def _():
        for i in range(iterate.shape[0]):
            value = updated(i, arrived, table, transfer, correction, terms)
            iterate[i] = value
            rounded[i] = value.astype(jnp.bfloat16)


def residual_body(low, table, loads, *refs):
    *sources, blocks, residual, sent = refs[: len(refs) - (low == 0)]

    @pl.when(is_fine(table))
    def _():
        if low == 0:
            extension = refs[-1]
            joined(sources, extension)
        else:
            (extension,) = sources
        for i in range(residual.shape[0]):
            value = loads[low + i] - gathered(extension, table, low + i, blocks)
            residual[i] = value
            sent[i] = value.astype(jnp.bfloat16)


def last_body(table, early, late, correction, start, end, iterate, transfer, out, total, scratch, leaves):
    rows, _, width = total.shape
    copies = [
        pltpu.make_async_copy(total.at[i], out.at[:, pl.ds(i * width, width)], leaves.at[i])
        for i in range(rows)
    ]

    @pl.when(is_fine(table))
    def _():
        joined((early, late), scratch)
        for i in range(rows):
            value = iterate[i] + correction[i]
            total[i] = value + gathered(scratch, table, i, transfer)
            copies[i].start()

    @pl.when(jnp.logical_not(is_fine(table)))
    def _():
        for i in range(rows):
            total[i] = row_of((start, end), i)
            copies[i].start()

    for copy in copies:
        copy.wait()


def local(loads, level_blocks, level_cols, smoother, transfer_blocks, transfer_cols, bound_rows):
    block_rows = level_cols.shape[1]
    width = level_blocks.shape[-1]
    load_cols = loads.shape[1]
    list_width = bound_rows.shape[-1]
    left_list, right_list, sibling_list = bound_rows[0, 0]
    blocks, smooth, transfer, loads = level_blocks[0], smoother[0], transfer_blocks[0], loads[0]

    def panels(count, kind):
        return jax.ShapeDtypeStruct((count, load_cols, width), kind)

    def held(count):
        return pltpu.VMEM((count, load_cols, width), jnp.bfloat16)

    wide, narrow = panels(block_rows, jnp.float32), panels(block_rows, jnp.bfloat16)
    early_rows = block_rows * 3 // 8
    late_rows = block_rows - early_rows
    listed = panels(list_width, jnp.bfloat16)
    extended = panels(block_rows + 3 * list_width, jnp.bfloat16)
    rowwise = pltpu.SemaphoreType.DMA((block_rows,))

    load_panels, sent = call(
        open_body, (wide, narrow), inside(loads), in_specs=[HBM], scratch=[rowwise],
        cost=pl.CostEstimate(flops=5_000_000_000, bytes_accessed=2 * loads.size * 4, transcendentals=0),
    )
    arrived = [partner(sent, "level", 1)]

    def spread(values):
        return jnp.broadcast_to(values[:, None], (values.shape[0], LANES))

    def swap_all(odd, others):
        behind = swapped(odd, "dom", 1)
        ahead, beside = others()
        ahead = swapped(ahead, "dom", 0)
        beside = partner(beside, "level", 0)
        return ahead, behind, beside

    even = lax.axis_index("dom") % 2 == 0
    wanted_even, wanted_odd, wanted_beside = swap_all(
        spread(jnp.where(even, left_list, right_list)),
        lambda: (spread(jnp.where(even, right_list, left_list)), spread(sibling_list)),
    )
    columns = level_cols.reshape(-1)
    from_left = (columns >= block_rows) & (columns < block_rows + list_width)
    from_right = (columns >= block_rows + list_width) & (columns < block_rows + 2 * list_width)
    moved = jnp.where(from_left, list_width, 0) - jnp.where(from_right, list_width, 0)
    columns = columns + jnp.where(even, moved, 0)
    fine = (lax.axis_index("level") < 2).astype(jnp.int32).reshape(1)

    level_table = spread(jnp.concatenate([columns, fine]))
    transfer_table = spread(jnp.concatenate([transfer_cols.reshape(-1), fine]))

    def fetched(source):
        return call(fetch_body, like(source), inside(loads), inside(source), in_specs=[HBM, HBM], scratch=[rowwise])

    def exchanged(body, fixed, pieces, rest, joins, scratch):
        def listed_rows(wanted, pieces, joins):
            lists, each = len(wanted), len(pieces[0])
            held_rows = [held(lists * list_width)] * scratch
            return call(
                lambda *refs: body(lists, each, *refs), (listed,) * lists + joins,
                *fixed, *wanted, *sum(pieces, []), *rest, scratch=held_rows,
            )

        odd, *whole = listed_rows([wanted_odd], pieces, joins)
        whole = whole or sum(pieces, [])
        sides = swap_all(odd, lambda: listed_rows([wanted_even, wanted_beside], [[x] for x in whole], ()))
        return whole, sides

    def part(rows):
        return panels(rows, jnp.float32), panels(rows, jnp.bfloat16)

    def sent_on(x):
        return partner(x, "level", 1)

    transfer = fetched(transfer)
    residual, iterate = [load_panels], None
    for cycle_index in range(ITERS):
        if cycle_index > 0:
            args = (level_table, load_panels)
            early, sent, extension = call(
                lambda *refs: residual_body(0, *refs), part(early_rows) + (extended,),
                *args, rounded, *sides, blocks,
            )
            arrived = [sent_on(sent)]
            late, sent = call(
                lambda *refs: residual_body(early_rows, *refs), part(late_rows),
                *args, extension, blocks,
            )
            arrived.append(partner(sent, "level", 1))
            residual = [early, late]
        args, rest = (transfer_table, load_panels), (transfer, smooth)
        whole, sides = exchanged(
            first_listed_body, args, [residual, arrived], rest,
            (wide, narrow) if len(arrived) > 1 else (), True,
        )
        current, first = call(first_body, (wide, narrow), *args, *whole, *rest)
        args = (level_table, current, first)
        ends = cycle_index + 1 == ITERS
        rounded, extension, *start = call(
            second_start_body,
            (panels(early_rows, jnp.bfloat16), extended) + (panels(early_rows, jnp.float32),) * ends,
            *args, *sides, blocks, smooth,
        )
        returned = [sent_on(rounded)]
        rounded, *end = call(
            second_end_body,
            (panels(late_rows, jnp.bfloat16),) + (panels(late_rows, jnp.float32),) * ends,
            *args, extension, blocks, smooth,
        )
        returned.append(sent_on(rounded))
        correction = call(second_fine_body, wide, *args, extension, blocks, smooth, scratch=[held(block_rows)])
        if not ends:
            rest = [correction] + ([] if iterate is None else [iterate]) + [transfer]
            whole, sides = exchanged(update_listed_body, (transfer_table,), [returned], rest, (narrow,), False)
            iterate, rounded = call(update_body, (wide, narrow), transfer_table, *whole, *rest)
    final = call(
        last_body, jax.ShapeDtypeStruct((load_cols, block_rows * width), jnp.float32),
        transfer_table, *returned, correction, *start, *end, iterate, transfer, out_specs=HBM,
        scratch=[pltpu.VMEM(wide.shape, jnp.float32), held(block_rows), rowwise],
    )
    return final[None]


def solution(mesh):
    in_specs = (
        P("level", None, "dom"),
        P("level", "dom", None, None, None),
        P("level", "dom", None),
        P("level", "dom", None, None),
        P("level", "dom", None, None, None),
        P("level", "dom", None),
        P("level", "dom", None, None),
    )
    out_specs = P("level", None, "dom")

    return jax.shard_map(local, mesh=mesh, in_specs=in_specs, out_specs=out_specs, check_vma=False)
```

```python
import jax
import jax.numpy as jnp
from jax import lax
from jax.experimental import pallas as pl
from jax.experimental.pallas import tpu as pltpu
from jax.sharding import PartitionSpec as P

ITERS = 2
LIMIT = 16 << 20
LANES = 128
SHARES = (0, 3, 11, 16)
VMEM = pl.BlockSpec(memory_space=pltpu.VMEM)
HBM = pl.BlockSpec(memory_space=pltpu.HBM)
NT = (((1,), (1,)), ((), ()))


def partner(x, axis, apart):
    return lax.ppermute(x, axis, [(i, i ^ 1 << apart) for i in range(lax.axis_size(axis))])


def swapped(x, axis, first):
    size = lax.axis_size(axis)
    pairs = [(i % size, (i + 1) % size) for i in range(first, first + size, 2)]
    return lax.ppermute(x, axis, pairs + [(b, a) for a, b in pairs])


def like(x):
    return jax.ShapeDtypeStruct(x.shape, x.dtype)


def inside(x):
    return pltpu.with_memory_space_constraint(x, pltpu.HBM)


def call(body, outs, *args, in_specs=None, out_specs=None, scratch=(), cost=None):
    if cost is None:
        size = sum(x.size * x.dtype.itemsize for x in (*args, *jax.tree.leaves(outs)))
        cost = pl.CostEstimate(flops=64 * size, bytes_accessed=size, transcendentals=0)
    return pl.pallas_call(
        body,
        out_shape=outs,
        in_specs=in_specs or [VMEM] * len(args),
        out_specs=out_specs or jax.tree.map(lambda _: VMEM, outs),
        scratch_shapes=list(scratch),
        cost_estimate=cost,
        compiler_params=pltpu.CompilerParams(vmem_limit_bytes=LIMIT),
    )(*args)


def entry(table, at):
    return table[pl.ds(at, 1), 0:1][0, 0]


def is_fine(table):
    return entry(table, table.shape[0] - 1) == 1


def times(panel, block):
    return lax.dot_general(panel, block, NT, preferred_element_type=jnp.float32)


def gathered(source, table, row, blocks):
    count = blocks.shape[1]
    left = jnp.concatenate([source[entry(table, row * count + k)] for k in range(count)], axis=1)
    right = jnp.concatenate([blocks[row, k] for k in range(count)], axis=1)
    return times(left, right)


def joined(parts, scratch):
    at = 0
    for part in parts:
        for i in range(part.shape[0]):
            scratch[at + i] = part[i]
        at += part.shape[0]


def open_body(loads, panels, sent, arrivals):
    rows, _, width = panels.shape
    copies = [
        pltpu.make_async_copy(
            loads.at[:, pl.ds(i * width, width)], panels.at[i], arrivals.at[i]
        )
        for i in range(rows)
    ]
    for copy in copies:
        copy.start()
    for i, copy in enumerate(copies):
        copy.wait()
        sent[i] = panels[i].astype(jnp.bfloat16)


def fetch_body(_, source, target, arrivals):
    copies = [
        pltpu.make_async_copy(source.at[i], target.at[i], arrivals.at[i])
        for i in range(source.shape[0])
    ]
    for copy in copies:
        copy.start()
    for copy in copies:
        copy.wait()


def chosen(wanted, outs):
    return [(entry(rows, j), out, j) for rows, out in zip(wanted, outs) for j in range(out.shape[0])]


def first_listed_body(lists, pieces, table, loads, *refs):
    wanted, refs = refs[:lists], refs[lists:]
    residual, arrived, refs = refs[:pieces], refs[pieces : 2 * pieces], refs[2 * pieces :]
    transfer, smoother, *refs, scratch = refs
    outs = refs[:lists]
    places = chosen(wanted, outs)
    if pieces > 1:
        joined_residual, joined_arrived = refs[lists:]
    else:
        (joined_residual,), (joined_arrived,) = residual, arrived

    @pl.when(is_fine(table))
    def _():
        if pieces > 1:
            joined(residual, joined_residual)
        for at, (row, _, _) in enumerate(places):
            scratch[at] = joined_residual[row].astype(jnp.bfloat16)

    @pl.when(jnp.logical_not(is_fine(table)))
    def _():
        if pieces > 1:
            joined(arrived, joined_arrived)
        for at, (row, _, _) in enumerate(places):
            value = loads[row] + gathered(joined_arrived, table, row, transfer)
            scratch[at] = value.astype(jnp.bfloat16)

    for at, (row, out, j) in enumerate(places):
        out[j] = times(scratch[at], smoother[row]).astype(jnp.bfloat16)


def first_body(table, loads, wanted, residual, arrived, transfer, smoother, current, first, beside):
    rows = first.shape[0]

    @pl.when(is_fine(table))
    def _():
        joined([residual], current)

    @pl.when(jnp.logical_not(is_fine(table)))
    def _():
        for i in range(rows):
            current[i] = loads[i] + gathered(arrived, table, i, transfer)

    for i in range(rows):
        value = times(current[i].astype(jnp.bfloat16), smoother[i])
        first[i] = value.astype(jnp.bfloat16)
    for row, out, j in chosen([wanted], [beside]):
        out[j] = first[row]


def second_rows(low, table, current, first, extension, blocks, smoother, rounded, full=None):
    rows = rounded.shape[0]
    for i in range(rows):
        applied = gathered(extension, table, low + i, blocks)
        rounded[i] = (current[low + i] - applied).astype(jnp.bfloat16)
    for i in range(rows):
        value = first[low + i].astype(jnp.float32) + times(rounded[i], smoother[low + i])
        rounded[i] = value.astype(jnp.bfloat16)
        if full is not None:
            full[i] = value


def second_start_body(low, table, current, first, left, right, sibling, blocks, smoother, rounded, extension, *full):
    joined([first, left, right, sibling], extension)

    @pl.when(jnp.logical_not(is_fine(table)))
    def _():
        second_rows(low, table, current, first, extension, blocks, smoother, rounded, *full)


def second_more_body(low, table, current, first, extension, blocks, smoother, rounded, *full):
    @pl.when(jnp.logical_not(is_fine(table)))
    def _():
        second_rows(low, table, current, first, extension, blocks, smoother, rounded, *full)


def second_fine_body(table, current, first, extension, blocks, smoother, full, scratch):
    @pl.when(is_fine(table))
    def _():
        second_rows(0, table, current, first, extension, blocks, smoother, scratch, full)


def row_of(parts, at):
    for part in parts:
        if at < part.shape[0]:
            return part[at]
        at -= part.shape[0]


def updated(row, arrived, table, transfer, correction, terms):
    value = correction[row]
    for term in terms:
        value = term[row] + value
    return value + gathered(arrived, table, row, transfer)


def update_listed_body(lists, pieces, table, *refs):
    wanted, arrived, refs = refs[:lists], refs[lists : lists + pieces], refs[lists + pieces :]
    more = lists + (pieces > 1)
    correction, *terms, transfer = refs[:-more]
    outs = refs[-more:][:lists]

    @pl.when(is_fine(table))
    def _():
        if pieces > 1:
            joined(arrived, refs[-1])
        source = refs[-1] if pieces > 1 else arrived[0]
        for row, out, j in chosen(wanted, outs):
            value = updated(row, source, table, transfer, correction, terms)
            out[j] = value.astype(jnp.bfloat16)


def update_body(table, wanted, arrived, correction, *refs):
    *terms, transfer, iterate, rounded, beside = refs

    @pl.when(is_fine(table))
    def _():
        for i in range(iterate.shape[0]):
            value = updated(i, arrived, table, transfer, correction, terms)
            iterate[i] = value
            rounded[i] = value.astype(jnp.bfloat16)
        for row, out, j in chosen([wanted], [beside]):
            out[j] = rounded[row]


def residual_rows(low, table, loads, extension, blocks, sent, residual):
    for i in range(residual.shape[0]):
        value = loads[low + i] - gathered(extension, table, low + i, blocks)
        residual[i] = value
        sent[i] = value.astype(jnp.bfloat16)


def residual_start_body(low, table, loads, own, left, right, sibling, blocks, sent, extension, residual):
    @pl.when(is_fine(table))
    def _():
        joined([own, left, right, sibling], extension)
        residual_rows(low, table, loads, extension, blocks, sent, residual)


def residual_more_body(low, table, loads, extension, blocks, sent, residual):
    @pl.when(is_fine(table))
    def _():
        residual_rows(low, table, loads, extension, blocks, sent, residual)


def last_body(table, *refs):
    *pieces, correction, iterate, transfer, out, total, scratch, leaves = refs
    arrived, finals = pieces[: len(pieces) // 2], pieces[len(pieces) // 2 :]
    rows, _, width = total.shape
    copies = [
        pltpu.make_async_copy(total.at[i], out.at[:, pl.ds(i * width, width)], leaves.at[i])
        for i in range(rows)
    ]

    @pl.when(is_fine(table))
    def _():
        joined(arrived, scratch)
        for i in range(rows):
            value = iterate[i] + correction[i]
            total[i] = value + gathered(scratch, table, i, transfer)
            copies[i].start()

    @pl.when(jnp.logical_not(is_fine(table)))
    def _():
        for i in range(rows):
            total[i] = row_of(finals, i)
            copies[i].start()

    for copy in copies:
        copy.wait()


def local(loads, level_blocks, level_cols, smoother, transfer_blocks, transfer_cols, bound_rows):
    block_rows = level_cols.shape[1]
    width = level_blocks.shape[-1]
    load_cols = loads.shape[1]
    list_width = bound_rows.shape[-1]
    left_list, right_list, sibling_list = bound_rows[0, 0]
    blocks, smooth, transfer, loads = level_blocks[0], smoother[0], transfer_blocks[0], loads[0]

    def panels(count, kind):
        return jax.ShapeDtypeStruct((count, load_cols, width), kind)

    def held(count):
        return pltpu.VMEM((count, load_cols, width), jnp.bfloat16)

    wide, narrow = panels(block_rows, jnp.float32), panels(block_rows, jnp.bfloat16)
    bounds = [block_rows * share // 16 for share in SHARES]
    parts = list(zip(bounds[:-1], bounds[1:]))
    listed = panels(list_width, jnp.bfloat16)
    extended = panels(block_rows + 3 * list_width, jnp.bfloat16)
    rowwise = pltpu.SemaphoreType.DMA((block_rows,))

    load_panels, sent = call(
        open_body, (wide, narrow), inside(loads), in_specs=[HBM], scratch=[rowwise],
        cost=pl.CostEstimate(flops=5_000_000_000, bytes_accessed=2 * loads.size * 4, transcendentals=0),
    )
    arrived = [partner(sent, "level", 1)]

    def spread(values):
        return jnp.broadcast_to(values[:, None], (values.shape[0], LANES))

    def swap_both(odd, even):
        odd = swapped(odd, "dom", 1)
        even = swapped(even, "dom", 0)
        return even, odd

    def swap_beside(x):
        return partner(x, "level", 0)

    even = lax.axis_index("dom") % 2 == 0
    wanted_even, wanted_odd = swap_both(
        spread(jnp.where(even, left_list, right_list)), spread(jnp.where(even, right_list, left_list))
    )
    wanted_beside = swap_beside(spread(sibling_list))
    columns = level_cols.reshape(-1)
    from_left = (columns >= block_rows) & (columns < block_rows + list_width)
    from_right = (columns >= block_rows + list_width) & (columns < block_rows + 2 * list_width)
    moved = jnp.where(from_left, list_width, 0) - jnp.where(from_right, list_width, 0)
    columns = columns + jnp.where(even, moved, 0)
    fine = (lax.axis_index("level") < 2).astype(jnp.int32).reshape(1)

    level_table = spread(jnp.concatenate([columns, fine]))
    transfer_table = spread(jnp.concatenate([transfer_cols.reshape(-1), fine]))

    def fetched(source):
        return call(fetch_body, like(source), inside(loads), inside(source), in_specs=[HBM, HBM], scratch=[rowwise])

    def exchanged(bodies, fixed, pieces, rest, joins, scratch):
        listed_body, body = bodies
        each = len(pieces[0])
        odd, even, *whole = call(
            lambda *refs: listed_body(2, each, *refs), (listed,) * 2 + joins,
            *fixed, wanted_odd, wanted_even, *sum(pieces, []), *rest,
            scratch=[held(2 * list_width)] * scratch,
        )
        even, odd = swap_both(odd, even)
        whole = whole or sum(pieces, [])
        *results, beside = call(body, (wide, narrow, listed), *fixed, wanted_beside, *whole, *rest)
        return (*results, (even, odd, swap_beside(beside)))

    def in_parts(body, more_body, args, sources, rest, wanted):
        kept, passed = [], []
        for at, (low, high) in enumerate(parts):
            outs = (panels(high - low, jnp.bfloat16),) + (extended,) * (at == 0)
            outs += (panels(high - low, jnp.float32),) * wanted
            rounded, *more = call(
                lambda *refs: (more_body if at else body)(low, *refs), outs,
                *args, *sources, *rest,
            )
            if at == 0:
                sources = [more.pop(0)]
            kept += more
            passed.append(partner(rounded, "level", 1))
        return passed, kept, sources[0]

    transfer = fetched(transfer)
    residual, iterate = [load_panels], None
    for cycle_index in range(ITERS):
        if cycle_index > 0:
            arrived, residual, _ = in_parts(
                residual_start_body, residual_more_body, (level_table, load_panels),
                (rounded, *sides), (blocks,), True,
            )
        args, rest = (transfer_table, load_panels), (transfer, smooth)
        current, first, sides = exchanged(
            (first_listed_body, first_body), args, [residual, arrived], rest,
            (wide, narrow) if len(arrived) > 1 else (), True,
        )
        args = (level_table, current, first)
        ends = cycle_index + 1 == ITERS
        returned, finals, extension = in_parts(second_start_body, second_more_body, args, sides, (blocks, smooth), ends)
        correction = call(second_fine_body, wide, *args, extension, blocks, smooth, scratch=[held(block_rows)])
        if not ends:
            rest = [correction] + ([] if iterate is None else [iterate]) + [transfer]
            iterate, rounded, sides = exchanged(
                (update_listed_body, update_body), (transfer_table,), [returned], rest,
                (narrow,), False,
            )
    final = call(
        last_body, jax.ShapeDtypeStruct((load_cols, block_rows * width), jnp.float32),
        transfer_table, *returned, *finals, correction, iterate, transfer, out_specs=HBM,
        scratch=[pltpu.VMEM(wide.shape, jnp.float32), held(block_rows), rowwise],
    )
    return final[None]


def solution(mesh):
    in_specs = (
        P("level", None, "dom"),
        P("level", "dom", None, None, None),
        P("level", "dom", None),
        P("level", "dom", None, None),
        P("level", "dom", None, None, None),
        P("level", "dom", None),
        P("level", "dom", None, None),
    )
    out_specs = P("level", None, "dom")

    return jax.shard_map(local, mesh=mesh, in_specs=in_specs, out_specs=out_specs, check_vma=False)
```

```python
import jax
import jax.numpy as jnp
from jax import lax
from jax.experimental import pallas as pl
from jax.experimental.pallas import tpu as pltpu
from jax.sharding import PartitionSpec as P

ITERS = 2
LIMIT = 16 << 20
LANES = 128
SHARES = (0, 6, 16)
VMEM = pl.BlockSpec(memory_space=pltpu.VMEM)
HBM = pl.BlockSpec(memory_space=pltpu.HBM)
NT = (((1,), (1,)), ((), ()))


def partner(x, axis, apart):
    return lax.ppermute(x, axis, [(i, i ^ 1 << apart) for i in range(lax.axis_size(axis))])


def swapped(x, axis, first):
    size = lax.axis_size(axis)
    pairs = [(i % size, (i + 1) % size) for i in range(first, first + size, 2)]
    return lax.ppermute(x, axis, pairs + [(b, a) for a, b in pairs])


def like(x):
    return jax.ShapeDtypeStruct(x.shape, x.dtype)


def inside(x):
    return pltpu.with_memory_space_constraint(x, pltpu.HBM)


def call(body, outs, *args, in_specs=None, out_specs=None, scratch=(), cost=None):
    if cost is None:
        size = sum(x.size * x.dtype.itemsize for x in (*args, *jax.tree.leaves(outs)))
        cost = pl.CostEstimate(flops=64 * size, bytes_accessed=size, transcendentals=0)
    return pl.pallas_call(
        body,
        out_shape=outs,
        in_specs=in_specs or [VMEM] * len(args),
        out_specs=out_specs or jax.tree.map(lambda _: VMEM, outs),
        scratch_shapes=list(scratch),
        cost_estimate=cost,
        compiler_params=pltpu.CompilerParams(vmem_limit_bytes=LIMIT),
    )(*args)


def entry(table, at):
    return table[pl.ds(at, 1), 0:1][0, 0]


def is_fine(table):
    return entry(table, table.shape[0] - 1) == 1


def times(panel, block):
    return lax.dot_general(panel, block, NT, preferred_element_type=jnp.float32)


def gathered(source, table, row, blocks):
    count = blocks.shape[1]
    left = jnp.concatenate([source[entry(table, row * count + k)] for k in range(count)], axis=1)
    right = jnp.concatenate([blocks[row, k] for k in range(count)], axis=1)
    return times(left, right)


def joined(parts, scratch):
    at = 0
    for part in parts:
        for i in range(part.shape[0]):
            scratch[at + i] = part[i]
        at += part.shape[0]


def open_body(loads, panels, early, late, arrivals):
    rows, _, width = panels.shape
    half = early.shape[0]
    copies = [
        pltpu.make_async_copy(
            loads.at[:, pl.ds(i * width, width)], panels.at[i], arrivals.at[i]
        )
        for i in range(rows)
    ]
    for copy in copies:
        copy.start()
    for i, copy in enumerate(copies):
        copy.wait()
        sent, at = (early, i) if i < half else (late, i - half)
        sent[at] = panels[i].astype(jnp.bfloat16)


def fetch_body(_, source, target, arrivals):
    copies = [
        pltpu.make_async_copy(source.at[i], target.at[i], arrivals.at[i])
        for i in range(source.shape[0])
    ]
    for copy in copies:
        copy.start()
    for copy in copies:
        copy.wait()


def chosen(wanted, outs):
    return [(entry(rows, j), out, j) for rows, out in zip(wanted, outs) for j in range(out.shape[0])]


def first_listed_body(lists, pieces, table, loads, *refs):
    wanted, refs = refs[:lists], refs[lists:]
    many, arrivals = pieces
    residual, arrived, refs = refs[:many], refs[many : many + arrivals], refs[many + arrivals :]
    transfer, smoother, *refs, scratch = refs
    outs, refs = refs[:lists], refs[lists:]
    places = chosen(wanted, outs)
    joined_residual = refs.pop(0) if many > 1 else residual[0]
    joined_arrived = refs.pop(0) if arrivals > 1 else arrived[0]

    @pl.when(is_fine(table))
    def _():
        if many > 1:
            joined(residual, joined_residual)
        for at, (row, _, _) in enumerate(places):
            scratch[at] = joined_residual[row].astype(jnp.bfloat16)

    @pl.when(jnp.logical_not(is_fine(table)))
    def _():
        if arrivals > 1:
            joined(arrived, joined_arrived)
        for at, (row, _, _) in enumerate(places):
            value = loads[row] + gathered(joined_arrived, table, row, transfer)
            scratch[at] = value.astype(jnp.bfloat16)

    for at, (row, out, j) in enumerate(places):
        out[j] = times(scratch[at], smoother[row]).astype(jnp.bfloat16)


def first_body(table, loads, wanted, residual, arrived, transfer, smoother, current, first, beside):
    rows = first.shape[0]

    @pl.when(is_fine(table))
    def _():
        joined([residual], current)

    @pl.when(jnp.logical_not(is_fine(table)))
    def _():
        for i in range(rows):
            current[i] = loads[i] + gathered(arrived, table, i, transfer)

    for i in range(rows):
        value = times(current[i].astype(jnp.bfloat16), smoother[i])
        first[i] = value.astype(jnp.bfloat16)
    for row, out, j in chosen([wanted], [beside]):
        out[j] = first[row]


def second_rows(low, table, current, first, extension, blocks, smoother, rounded, full=None):
    rows = rounded.shape[0]
    for i in range(rows):
        applied = gathered(extension, table, low + i, blocks)
        rounded[i] = (current[low + i] - applied).astype(jnp.bfloat16)
    for i in range(rows):
        value = first[low + i].astype(jnp.float32) + times(rounded[i], smoother[low + i])
        rounded[i] = value.astype(jnp.bfloat16)
        if full is not None:
            full[i] = value


def second_start_body(low, table, current, first, left, right, sibling, blocks, smoother, rounded, extension, *full):
    joined([first, left, right, sibling], extension)

    @pl.when(jnp.logical_not(is_fine(table)))
    def _():
        second_rows(low, table, current, first, extension, blocks, smoother, rounded, *full)


def second_more_body(low, table, current, first, extension, blocks, smoother, rounded, *full):
    @pl.when(jnp.logical_not(is_fine(table)))
    def _():
        second_rows(low, table, current, first, extension, blocks, smoother, rounded, *full)


def second_fine_body(table, current, first, extension, blocks, smoother, full, scratch):
    @pl.when(is_fine(table))
    def _():
        second_rows(0, table, current, first, extension, blocks, smoother, scratch, full)


def row_of(parts, at):
    for part in parts:
        if at < part.shape[0]:
            return part[at]
        at -= part.shape[0]


def updated(row, arrived, table, transfer, correction, terms):
    value = correction[row]
    for term in terms:
        value = term[row] + value
    return value + gathered(arrived, table, row, transfer)


def update_listed_body(lists, counts, table, *refs):
    (pieces,) = counts
    wanted, arrived, refs = refs[:lists], refs[lists : lists + pieces], refs[lists + pieces :]
    more = lists + (pieces > 1)
    correction, *terms, transfer = refs[:-more]
    outs = refs[-more:][:lists]

    @pl.when(is_fine(table))
    def _():
        if pieces > 1:
            joined(arrived, refs[-1])
        source = refs[-1] if pieces > 1 else arrived[0]
        for row, out, j in chosen(wanted, outs):
            value = updated(row, source, table, transfer, correction, terms)
            out[j] = value.astype(jnp.bfloat16)


def update_body(table, wanted, arrived, correction, *refs):
    *terms, transfer, iterate, rounded, beside = refs

    @pl.when(is_fine(table))
    def _():
        for i in range(iterate.shape[0]):
            value = updated(i, arrived, table, transfer, correction, terms)
            iterate[i] = value
            rounded[i] = value.astype(jnp.bfloat16)
        for row, out, j in chosen([wanted], [beside]):
            out[j] = rounded[row]


def residual_rows(low, table, loads, extension, blocks, sent, residual):
    for i in range(residual.shape[0]):
        value = loads[low + i] - gathered(extension, table, low + i, blocks)
        residual[i] = value
        sent[i] = value.astype(jnp.bfloat16)


def residual_start_body(low, table, loads, own, left, right, sibling, blocks, sent, extension, residual):
    @pl.when(is_fine(table))
    def _():
        joined([own, left, right, sibling], extension)
        residual_rows(low, table, loads, extension, blocks, sent, residual)


def residual_more_body(low, table, loads, extension, blocks, sent, residual):
    @pl.when(is_fine(table))
    def _():
        residual_rows(low, table, loads, extension, blocks, sent, residual)


def last_body(table, *refs):
    *pieces, correction, iterate, transfer, out, total, scratch, leaves = refs
    arrived, finals = pieces[: len(pieces) // 2], pieces[len(pieces) // 2 :]
    rows, _, width = total.shape
    copies = [
        pltpu.make_async_copy(total.at[i], out.at[:, pl.ds(i * width, width)], leaves.at[i])
        for i in range(rows)
    ]

    @pl.when(is_fine(table))
    def _():
        joined(arrived, scratch)
        for i in range(rows):
            value = iterate[i] + correction[i]
            total[i] = value + gathered(scratch, table, i, transfer)
            copies[i].start()

    @pl.when(jnp.logical_not(is_fine(table)))
    def _():
        for i in range(rows):
            total[i] = row_of(finals, i)
            copies[i].start()

    for copy in copies:
        copy.wait()


def local(loads, level_blocks, level_cols, smoother, transfer_blocks, transfer_cols, bound_rows):
    block_rows = level_cols.shape[1]
    width = level_blocks.shape[-1]
    load_cols = loads.shape[1]
    list_width = bound_rows.shape[-1]
    left_list, right_list, sibling_list = bound_rows[0, 0]
    blocks, smooth, transfer, loads = level_blocks[0], smoother[0], transfer_blocks[0], loads[0]

    def panels(count, kind):
        return jax.ShapeDtypeStruct((count, load_cols, width), kind)

    def held(count):
        return pltpu.VMEM((count, load_cols, width), jnp.bfloat16)

    wide, narrow = panels(block_rows, jnp.float32), panels(block_rows, jnp.bfloat16)
    bounds = [block_rows * share // 16 for share in SHARES]
    parts = list(zip(bounds[:-1], bounds[1:]))
    listed = panels(list_width, jnp.bfloat16)
    extended = panels(block_rows + 3 * list_width, jnp.bfloat16)
    rowwise = pltpu.SemaphoreType.DMA((block_rows,))

    half = panels(block_rows // 2, jnp.bfloat16)
    load_panels, *sent = call(
        open_body, (wide, half, half), inside(loads), in_specs=[HBM], scratch=[rowwise],
        cost=pl.CostEstimate(flops=5_000_000_000, bytes_accessed=2 * loads.size * 4, transcendentals=0),
    )
    arrived = []
    for piece in sent:
        arrived.append(partner(piece, "level", 1))

    def spread(values):
        return jnp.broadcast_to(values[:, None], (values.shape[0], LANES))

    def swap_both(odd, even):
        odd = swapped(odd, "dom", 1)
        even = even()
        even = swapped(even, "dom", 0)
        return even, odd

    def swap_beside(x):
        return partner(x, "level", 0)

    even = lax.axis_index("dom") % 2 == 0
    wanted_even, wanted_odd = swap_both(
        spread(jnp.where(even, left_list, right_list)), lambda: spread(jnp.where(even, right_list, left_list))
    )
    wanted_beside = swap_beside(spread(sibling_list))
    columns = level_cols.reshape(-1)
    from_left = (columns >= block_rows) & (columns < block_rows + list_width)
    from_right = (columns >= block_rows + list_width) & (columns < block_rows + 2 * list_width)
    moved = jnp.where(from_left, list_width, 0) - jnp.where(from_right, list_width, 0)
    columns = columns + jnp.where(even, moved, 0)
    fine = (lax.axis_index("level") < 2).astype(jnp.int32).reshape(1)

    level_table = spread(jnp.concatenate([columns, fine]))
    transfer_table = spread(jnp.concatenate([transfer_cols.reshape(-1), fine]))

    def fetched(source):
        return call(fetch_body, like(source), inside(loads), inside(source), in_specs=[HBM, HBM], scratch=[rowwise])

    def exchanged(bodies, fixed, pieces, rest, kinds, scratch):
        listed_body, body = bodies

        def listed_rows(wanted, pieces):
            counts = [len(x) for x in pieces]
            joins = tuple(kind for kind, count in zip(kinds, counts) if count > 1)
            out, *more = call(
                lambda *refs: listed_body(1, counts, *refs), (listed,) + joins,
                *fixed, wanted, *sum(pieces, []), *rest, scratch=[held(list_width)] * scratch,
            )
            return out, [more.pop(0) if count > 1 else x[0] for x, count in zip(pieces, counts)]

        odd, whole = listed_rows(wanted_odd, pieces)
        even, odd = swap_both(odd, lambda: listed_rows(wanted_even, [[x] for x in whole])[0])
        *results, beside = call(body, (wide, narrow, listed), *fixed, wanted_beside, *whole, *rest)
        return (*results, (even, odd, swap_beside(beside)))

    def in_parts(body, more_body, args, sources, rest, wanted):
        kept, passed = [], []
        for at, (low, high) in enumerate(parts):
            outs = (panels(high - low, jnp.bfloat16),) + (extended,) * (at == 0)
            outs += (panels(high - low, jnp.float32),) * wanted
            rounded, *more = call(
                lambda *refs: (more_body if at else body)(low, *refs), outs,
                *args, *sources, *rest,
            )
            if at == 0:
                sources = [more.pop(0)]
            kept += more
            passed.append(partner(rounded, "level", 1))
        return passed, kept, sources[0]

    transfer = fetched(transfer)
    residual, iterate = [load_panels], None
    for cycle_index in range(ITERS):
        if cycle_index > 0:
            arrived, residual, _ = in_parts(
                residual_start_body, residual_more_body, (level_table, load_panels),
                (rounded, *sides), (blocks,), True,
            )
        args, rest = (transfer_table, load_panels), (transfer, smooth)
        current, first, sides = exchanged(
            (first_listed_body, first_body), args, [residual, arrived], rest,
            (wide, narrow), True,
        )
        args = (level_table, current, first)
        ends = cycle_index + 1 == ITERS
        returned, finals, extension = in_parts(second_start_body, second_more_body, args, sides, (blocks, smooth), ends)
        correction = call(second_fine_body, wide, *args, extension, blocks, smooth, scratch=[held(block_rows)])
        if not ends:
            rest = [correction] + ([] if iterate is None else [iterate]) + [transfer]
            iterate, rounded, sides = exchanged(
                (update_listed_body, update_body), (transfer_table,), [returned], rest,
                (narrow,), False,
            )
    final = call(
        last_body, jax.ShapeDtypeStruct((load_cols, block_rows * width), jnp.float32),
        transfer_table, *returned, *finals, correction, iterate, transfer, out_specs=HBM,
        scratch=[pltpu.VMEM(wide.shape, jnp.float32), held(block_rows), rowwise],
    )
    return final[None]


def solution(mesh):
    in_specs = (
        P("level", None, "dom"),
        P("level", "dom", None, None, None),
        P("level", "dom", None),
        P("level", "dom", None, None),
        P("level", "dom", None, None, None),
        P("level", "dom", None),
        P("level", "dom", None, None),
    )
    out_specs = P("level", None, "dom")

    return jax.shard_map(local, mesh=mesh, in_specs=in_specs, out_specs=out_specs, check_vma=False)
```

```python
import jax
import jax.numpy as jnp
from jax import lax
from jax.experimental import pallas as pl
from jax.experimental.pallas import tpu as pltpu
from jax.sharding import PartitionSpec as P

ITERS = 2
LIMIT = 16 << 20
LANES = 128
VMEM = pl.BlockSpec(memory_space=pltpu.VMEM)
HBM = pl.BlockSpec(memory_space=pltpu.HBM)
NT = (((1,), (1,)), ((), ()))


def partner(x, axis, apart):
    return lax.ppermute(x, axis, [(i, i ^ 1 << apart) for i in range(lax.axis_size(axis))])


def swapped(x, axis, first):
    size = lax.axis_size(axis)
    pairs = [(i % size, (i + 1) % size) for i in range(first, first + size, 2)]
    return lax.ppermute(x, axis, pairs + [(b, a) for a, b in pairs])


def like(x):
    return jax.ShapeDtypeStruct(x.shape, x.dtype)


def inside(x):
    return pltpu.with_memory_space_constraint(x, pltpu.HBM)


def call(body, outs, *args, in_specs=None, out_specs=None, scratch=(), cost=None):
    if cost is None:
        size = sum(x.size * x.dtype.itemsize for x in (*args, *jax.tree.leaves(outs)))
        cost = pl.CostEstimate(flops=64 * size, bytes_accessed=size, transcendentals=0)
    return pl.pallas_call(
        body,
        out_shape=outs,
        in_specs=in_specs or [VMEM] * len(args),
        out_specs=out_specs or jax.tree.map(lambda _: VMEM, outs),
        scratch_shapes=list(scratch),
        cost_estimate=cost,
        compiler_params=pltpu.CompilerParams(vmem_limit_bytes=LIMIT),
    )(*args)


def entry(table, at):
    return table[pl.ds(at, 1), 0:1][0, 0]


def is_fine(table):
    return entry(table, table.shape[0] - 1) == 1


def times(panel, block):
    return lax.dot_general(panel, block, NT, preferred_element_type=jnp.float32)


def gathered(source, table, row, blocks):
    count = blocks.shape[1]
    left = jnp.concatenate([source[entry(table, row * count + k)] for k in range(count)], axis=1)
    right = jnp.concatenate([blocks[row, k] for k in range(count)], axis=1)
    return times(left, right)


def joined(parts, scratch):
    at = 0
    for part in parts:
        for i in range(part.shape[0]):
            scratch[at + i] = part[i]
        at += part.shape[0]


def open_body(loads, panels, sent, arrivals):
    rows, _, width = panels.shape
    copies = [
        pltpu.make_async_copy(
            loads.at[:, pl.ds(i * width, width)], panels.at[i], arrivals.at[i]
        )
        for i in range(rows)
    ]
    for copy in copies:
        copy.start()
    for i, copy in enumerate(copies):
        copy.wait()
        sent[i] = panels[i].astype(jnp.bfloat16)


def fetch_body(_, source, target, arrivals):
    copies = [
        pltpu.make_async_copy(source.at[i], target.at[i], arrivals.at[i])
        for i in range(source.shape[0])
    ]
    for copy in copies:
        copy.start()
    for copy in copies:
        copy.wait()


def chosen(wanted, outs):
    return [(entry(rows, j), out, j) for rows, out in zip(wanted, outs) for j in range(out.shape[0])]


def first_listed_body(lists, pieces, table, loads, *refs):
    wanted, refs = refs[:lists], refs[lists:]
    residual, arrived, refs = refs[:pieces], refs[pieces : 2 * pieces], refs[2 * pieces :]
    transfer, smoother, *refs, scratch = refs
    outs = refs[:lists]
    places = chosen(wanted, outs)
    if pieces > 1:
        joined_residual, joined_arrived = refs[lists:]
    else:
        (joined_residual,), (joined_arrived,) = residual, arrived

    @pl.when(is_fine(table))
    def _():
        if pieces > 1:
            joined(residual, joined_residual)
        for at, (row, _, _) in enumerate(places):
            scratch[at] = joined_residual[row].astype(jnp.bfloat16)

    @pl.when(jnp.logical_not(is_fine(table)))
    def _():
        if pieces > 1:
            joined(arrived, joined_arrived)
        for at, (row, _, _) in enumerate(places):
            value = loads[row] + gathered(joined_arrived, table, row, transfer)
            scratch[at] = value.astype(jnp.bfloat16)

    for at, (row, out, j) in enumerate(places):
        out[j] = times(scratch[at], smoother[row]).astype(jnp.bfloat16)


def first_body(table, loads, wanted, residual, arrived, transfer, smoother, current, first, beside):
    rows = first.shape[0]

    @pl.when(is_fine(table))
    def _():
        joined([residual], current)

    @pl.when(jnp.logical_not(is_fine(table)))
    def _():
        for i in range(rows):
            current[i] = loads[i] + gathered(arrived, table, i, transfer)

    for i in range(rows):
        value = times(current[i].astype(jnp.bfloat16), smoother[i])
        first[i] = value.astype(jnp.bfloat16)
    for row, out, j in chosen([wanted], [beside]):
        out[j] = first[row]


def second_rows(low, table, current, first, extension, blocks, smoother, rounded, full=None):
    rows = rounded.shape[0]
    for i in range(rows):
        applied = gathered(extension, table, low + i, blocks)
        rounded[i] = (current[low + i] - applied).astype(jnp.bfloat16)
    for i in range(rows):
        value = first[low + i].astype(jnp.float32) + times(rounded[i], smoother[low + i])
        rounded[i] = value.astype(jnp.bfloat16)
        if full is not None:
            full[i] = value


def second_start_body(table, current, first, left, right, sibling, blocks, smoother, rounded, extension, *full):
    joined([first, left, right, sibling], extension)

    @pl.when(jnp.logical_not(is_fine(table)))
    def _():
        second_rows(0, table, current, first, extension, blocks, smoother, rounded, *full)


def second_end_body(table, current, first, extension, blocks, smoother, rounded, *full):
    @pl.when(jnp.logical_not(is_fine(table)))
    def _():
        low = first.shape[0] - rounded.shape[0]
        second_rows(low, table, current, first, extension, blocks, smoother, rounded, *full)


def second_fine_body(table, current, first, extension, blocks, smoother, full, scratch):
    @pl.when(is_fine(table))
    def _():
        second_rows(0, table, current, first, extension, blocks, smoother, scratch, full)


def row_of(parts, at):
    for part in parts:
        if at < part.shape[0]:
            return part[at]
        at -= part.shape[0]


def updated(row, arrived, table, transfer, correction, terms):
    value = correction[row]
    for term in terms:
        value = term[row] + value
    return value + gathered(arrived, table, row, transfer)


def update_listed_body(lists, pieces, table, *refs):
    wanted, arrived, refs = refs[:lists], refs[lists : lists + pieces], refs[lists + pieces :]
    more = lists + (pieces > 1)
    correction, *terms, transfer = refs[:-more]
    outs = refs[-more:][:lists]

    @pl.when(is_fine(table))
    def _():
        if pieces > 1:
            joined(arrived, refs[-1])
        source = refs[-1] if pieces > 1 else arrived[0]
        for row, out, j in chosen(wanted, outs):
            value = updated(row, source, table, transfer, correction, terms)
            out[j] = value.astype(jnp.bfloat16)


def update_body(table, wanted, arrived, correction, *refs):
    *terms, transfer, iterate, rounded, beside = refs

    @pl.when(is_fine(table))
    def _():
        for i in range(iterate.shape[0]):
            value = updated(i, arrived, table, transfer, correction, terms)
            iterate[i] = value
            rounded[i] = value.astype(jnp.bfloat16)
        for row, out, j in chosen([wanted], [beside]):
            out[j] = rounded[row]


def residual_body(low, table, loads, *refs):
    *sources, blocks, residual, sent = refs[: len(refs) - (low == 0)]

    @pl.when(is_fine(table))
    def _():
        if low == 0:
            extension = refs[-1]
            joined(sources, extension)
        else:
            (extension,) = sources
        for i in range(residual.shape[0]):
            value = loads[low + i] - gathered(extension, table, low + i, blocks)
            residual[i] = value
            sent[i] = value.astype(jnp.bfloat16)


def last_body(table, early, late, correction, start, end, iterate, transfer, out, total, scratch, leaves):
    rows, _, width = total.shape
    copies = [
        pltpu.make_async_copy(total.at[i], out.at[:, pl.ds(i * width, width)], leaves.at[i])
        for i in range(rows)
    ]

    @pl.when(is_fine(table))
    def _():
        joined((early, late), scratch)
        for i in range(rows):
            value = iterate[i] + correction[i]
            total[i] = value + gathered(scratch, table, i, transfer)
            copies[i].start()

    @pl.when(jnp.logical_not(is_fine(table)))
    def _():
        for i in range(rows):
            total[i] = row_of((start, end), i)
            copies[i].start()

    for copy in copies:
        copy.wait()


def local(loads, level_blocks, level_cols, smoother, transfer_blocks, transfer_cols, bound_rows):
    block_rows = level_cols.shape[1]
    width = level_blocks.shape[-1]
    load_cols = loads.shape[1]
    list_width = bound_rows.shape[-1]
    left_list, right_list, sibling_list = bound_rows[0, 0]
    blocks, smooth, transfer, loads = level_blocks[0], smoother[0], transfer_blocks[0], loads[0]

    def panels(count, kind):
        return jax.ShapeDtypeStruct((count, load_cols, width), kind)

    def held(count):
        return pltpu.VMEM((count, load_cols, width), jnp.bfloat16)

    wide, narrow = panels(block_rows, jnp.float32), panels(block_rows, jnp.bfloat16)
    early_rows = block_rows // 2
    late_rows = block_rows - early_rows
    listed = panels(list_width, jnp.bfloat16)
    extended = panels(block_rows + 3 * list_width, jnp.bfloat16)
    rowwise = pltpu.SemaphoreType.DMA((block_rows,))

    load_panels, sent = call(
        open_body, (wide, narrow), inside(loads), in_specs=[HBM], scratch=[rowwise],
        cost=pl.CostEstimate(flops=5_000_000_000, bytes_accessed=2 * loads.size * 4, transcendentals=0),
    )
    arrived = [partner(sent, "level", 1)]

    def spread(values):
        return jnp.broadcast_to(values[:, None], (values.shape[0], LANES))

    def swap_both(odd, even):
        odd = swapped(odd, "dom", 1)
        even = swapped(even, "dom", 0)
        return even, odd

    def swap_beside(x):
        return partner(x, "level", 0)

    even = lax.axis_index("dom") % 2 == 0
    wanted_even, wanted_odd = swap_both(
        spread(jnp.where(even, left_list, right_list)), spread(jnp.where(even, right_list, left_list))
    )
    wanted_beside = swap_beside(spread(sibling_list))
    columns = level_cols.reshape(-1)
    from_left = (columns >= block_rows) & (columns < block_rows + list_width)
    from_right = (columns >= block_rows + list_width) & (columns < block_rows + 2 * list_width)
    moved = jnp.where(from_left, list_width, 0) - jnp.where(from_right, list_width, 0)
    columns = columns + jnp.where(even, moved, 0)
    fine = (lax.axis_index("level") < 2).astype(jnp.int32).reshape(1)

    level_table = spread(jnp.concatenate([columns, fine]))
    transfer_table = spread(jnp.concatenate([transfer_cols.reshape(-1), fine]))

    def fetched(source):
        return call(fetch_body, like(source), inside(loads), inside(source), in_specs=[HBM, HBM], scratch=[rowwise])

    def exchanged(bodies, fixed, pieces, rest, joins, scratch):
        listed_body, body = bodies
        each = len(pieces[0])
        odd, even, *whole = call(
            lambda *refs: listed_body(2, each, *refs), (listed,) * 2 + joins,
            *fixed, wanted_odd, wanted_even, *sum(pieces, []), *rest,
            scratch=[held(2 * list_width)] * scratch,
        )
        even, odd = swap_both(odd, even)
        whole = whole or sum(pieces, [])
        *results, beside = call(body, (wide, narrow, listed), *fixed, wanted_beside, *whole, *rest)
        return (*results, (even, odd, swap_beside(beside)))

    def part(rows):
        return panels(rows, jnp.float32), panels(rows, jnp.bfloat16)

    def sent_on(x):
        return partner(x, "level", 1)

    transfer = fetched(transfer)
    residual, iterate = [load_panels], None
    for cycle_index in range(ITERS):
        if cycle_index > 0:
            args = (level_table, load_panels)
            early, sent, extension = call(
                lambda *refs: residual_body(0, *refs), part(early_rows) + (extended,),
                *args, rounded, *sides, blocks,
            )
            arrived = [sent_on(sent)]
            late, sent = call(
                lambda *refs: residual_body(early_rows, *refs), part(late_rows),
                *args, extension, blocks,
            )
            arrived.append(partner(sent, "level", 1))
            residual = [early, late]
        args, rest = (transfer_table, load_panels), (transfer, smooth)
        current, first, sides = exchanged(
            (first_listed_body, first_body), args, [residual, arrived], rest,
            (wide, narrow) if len(arrived) > 1 else (), True,
        )
        args = (level_table, current, first)
        ends = cycle_index + 1 == ITERS
        rounded, extension, *start = call(
            second_start_body,
            (panels(early_rows, jnp.bfloat16), extended) + (panels(early_rows, jnp.float32),) * ends,
            *args, *sides, blocks, smooth,
        )
        returned = [sent_on(rounded)]
        rounded, *end = call(
            second_end_body,
            (panels(late_rows, jnp.bfloat16),) + (panels(late_rows, jnp.float32),) * ends,
            *args, extension, blocks, smooth,
        )
        returned.append(sent_on(rounded))
        correction = call(second_fine_body, wide, *args, extension, blocks, smooth, scratch=[held(block_rows)])
        if not ends:
            rest = [correction] + ([] if iterate is None else [iterate]) + [transfer]
            iterate, rounded, sides = exchanged(
                (update_listed_body, update_body), (transfer_table,), [returned], rest,
                (narrow,), False,
            )
    final = call(
        last_body, jax.ShapeDtypeStruct((load_cols, block_rows * width), jnp.float32),
        transfer_table, *returned, correction, *start, *end, iterate, transfer, out_specs=HBM,
        scratch=[pltpu.VMEM(wide.shape, jnp.float32), held(block_rows), rowwise],
    )
    return final[None]


def solution(mesh):
    in_specs = (
        P("level", None, "dom"),
        P("level", "dom", None, None, None),
        P("level", "dom", None),
        P("level", "dom", None, None),
        P("level", "dom", None, None, None),
        P("level", "dom", None),
        P("level", "dom", None, None),
    )
    out_specs = P("level", None, "dom")

    return jax.shard_map(local, mesh=mesh, in_specs=in_specs, out_specs=out_specs, check_vma=False)
```

```python
import jax
import jax.numpy as jnp
from jax import lax
from jax.experimental import pallas as pl
from jax.experimental.pallas import tpu as pltpu
from jax.sharding import PartitionSpec as P

ITERS = 2
LIMIT = 16 << 20
LANES = 128
SHARES = (0, 8, 16)
VMEM = pl.BlockSpec(memory_space=pltpu.VMEM)
HBM = pl.BlockSpec(memory_space=pltpu.HBM)
NT = (((1,), (1,)), ((), ()))


def partner(x, axis, apart):
    return lax.ppermute(x, axis, [(i, i ^ 1 << apart) for i in range(lax.axis_size(axis))])


def swapped(x, axis, first):
    size = lax.axis_size(axis)
    pairs = [(i % size, (i + 1) % size) for i in range(first, first + size, 2)]
    return lax.ppermute(x, axis, pairs + [(b, a) for a, b in pairs])


def like(x):
    return jax.ShapeDtypeStruct(x.shape, x.dtype)


def inside(x):
    return pltpu.with_memory_space_constraint(x, pltpu.HBM)


def call(body, outs, *args, in_specs=None, out_specs=None, scratch=(), cost=None):
    if cost is None:
        size = sum(x.size * x.dtype.itemsize for x in (*args, *jax.tree.leaves(outs)))
        cost = pl.CostEstimate(flops=64 * size, bytes_accessed=size, transcendentals=0)
    return pl.pallas_call(
        body,
        out_shape=outs,
        in_specs=in_specs or [VMEM] * len(args),
        out_specs=out_specs or jax.tree.map(lambda _: VMEM, outs),
        scratch_shapes=list(scratch),
        cost_estimate=cost,
        compiler_params=pltpu.CompilerParams(vmem_limit_bytes=LIMIT),
    )(*args)


def entry(table, at):
    return table[pl.ds(at, 1), 0:1][0, 0]


def is_fine(table):
    return entry(table, table.shape[0] - 1) == 1


def times(panel, block):
    return lax.dot_general(panel, block, NT, preferred_element_type=jnp.float32)


def gathered(source, table, row, blocks):
    count = blocks.shape[1]
    left = jnp.concatenate([source[entry(table, row * count + k)] for k in range(count)], axis=1)
    right = jnp.concatenate([blocks[row, k] for k in range(count)], axis=1)
    return times(left, right)


def joined(parts, scratch):
    at = 0
    for part in parts:
        for i in range(part.shape[0]):
            scratch[at + i] = part[i]
        at += part.shape[0]


def open_body(loads, panels, sent, arrivals):
    rows, _, width = panels.shape
    copies = [
        pltpu.make_async_copy(
            loads.at[:, pl.ds(i * width, width)], panels.at[i], arrivals.at[i]
        )
        for i in range(rows)
    ]
    for copy in copies:
        copy.start()
    for i, copy in enumerate(copies):
        copy.wait()
        sent[i] = panels[i].astype(jnp.bfloat16)


def fetch_body(_, source, target, arrivals):
    copies = [
        pltpu.make_async_copy(source.at[i], target.at[i], arrivals.at[i])
        for i in range(source.shape[0])
    ]
    for copy in copies:
        copy.start()
    for copy in copies:
        copy.wait()


def chosen(wanted, outs):
    return [(entry(rows, j), out, j) for rows, out in zip(wanted, outs) for j in range(out.shape[0])]


def first_listed_body(lists, pieces, table, loads, *refs):
    wanted, refs = refs[:lists], refs[lists:]
    residual, arrived, refs = refs[:pieces], refs[pieces : 2 * pieces], refs[2 * pieces :]
    transfer, smoother, *refs, scratch = refs
    outs = refs[:lists]
    places = chosen(wanted, outs)
    if pieces > 1:
        joined_residual, joined_arrived = refs[lists:]
    else:
        (joined_residual,), (joined_arrived,) = residual, arrived

    @pl.when(is_fine(table))
    def _():
        if pieces > 1:
            joined(residual, joined_residual)
        for at, (row, _, _) in enumerate(places):
            scratch[at] = joined_residual[row].astype(jnp.bfloat16)

    @pl.when(jnp.logical_not(is_fine(table)))
    def _():
        if pieces > 1:
            joined(arrived, joined_arrived)
        for at, (row, _, _) in enumerate(places):
            value = loads[row] + gathered(joined_arrived, table, row, transfer)
            scratch[at] = value.astype(jnp.bfloat16)

    for at, (row, out, j) in enumerate(places):
        out[j] = times(scratch[at], smoother[row]).astype(jnp.bfloat16)


def first_body(table, loads, wanted, residual, arrived, transfer, smoother, current, first, beside):
    rows = first.shape[0]

    @pl.when(is_fine(table))
    def _():
        joined([residual], current)

    @pl.when(jnp.logical_not(is_fine(table)))
    def _():
        for i in range(rows):
            current[i] = loads[i] + gathered(arrived, table, i, transfer)

    for i in range(rows):
        value = times(current[i].astype(jnp.bfloat16), smoother[i])
        first[i] = value.astype(jnp.bfloat16)
    for row, out, j in chosen([wanted], [beside]):
        out[j] = first[row]


def second_rows(low, table, current, first, extension, blocks, smoother, rounded, full=None):
    rows = rounded.shape[0]
    for i in range(rows):
        applied = gathered(extension, table, low + i, blocks)
        rounded[i] = (current[low + i] - applied).astype(jnp.bfloat16)
    for i in range(rows):
        value = first[low + i].astype(jnp.float32) + times(rounded[i], smoother[low + i])
        rounded[i] = value.astype(jnp.bfloat16)
        if full is not None:
            full[i] = value


def second_start_body(low, table, current, first, left, right, sibling, blocks, smoother, rounded, extension, *full):
    joined([first, left, right, sibling], extension)

    @pl.when(jnp.logical_not(is_fine(table)))
    def _():
        second_rows(low, table, current, first, extension, blocks, smoother, rounded, *full)


def second_more_body(low, table, current, first, extension, blocks, smoother, rounded, *full):
    @pl.when(jnp.logical_not(is_fine(table)))
    def _():
        second_rows(low, table, current, first, extension, blocks, smoother, rounded, *full)


def second_fine_body(table, current, first, extension, blocks, smoother, full, scratch):
    @pl.when(is_fine(table))
    def _():
        second_rows(0, table, current, first, extension, blocks, smoother, scratch, full)


def row_of(parts, at):
    for part in parts:
        if at < part.shape[0]:
            return part[at]
        at -= part.shape[0]


def updated(row, arrived, table, transfer, correction, terms):
    value = correction[row]
    for term in terms:
        value = term[row] + value
    return value + gathered(arrived, table, row, transfer)


def update_listed_body(lists, pieces, table, *refs):
    wanted, arrived, refs = refs[:lists], refs[lists : lists + pieces], refs[lists + pieces :]
    more = lists + (pieces > 1)
    correction, *terms, transfer = refs[:-more]
    outs = refs[-more:][:lists]

    @pl.when(is_fine(table))
    def _():
        if pieces > 1:
            joined(arrived, refs[-1])
        source = refs[-1] if pieces > 1 else arrived[0]
        for row, out, j in chosen(wanted, outs):
            value = updated(row, source, table, transfer, correction, terms)
            out[j] = value.astype(jnp.bfloat16)


def update_body(table, wanted, arrived, correction, *refs):
    *terms, transfer, iterate, rounded, beside = refs

    @pl.when(is_fine(table))
    def _():
        for i in range(iterate.shape[0]):
            value = updated(i, arrived, table, transfer, correction, terms)
            iterate[i] = value
            rounded[i] = value.astype(jnp.bfloat16)
        for row, out, j in chosen([wanted], [beside]):
            out[j] = rounded[row]


def residual_rows(low, table, loads, extension, blocks, sent, residual):
    for i in range(residual.shape[0]):
        value = loads[low + i] - gathered(extension, table, low + i, blocks)
        residual[i] = value
        sent[i] = value.astype(jnp.bfloat16)


def residual_start_body(low, table, loads, own, left, right, sibling, blocks, sent, extension, residual):
    @pl.when(is_fine(table))
    def _():
        joined([own, left, right, sibling], extension)
        residual_rows(low, table, loads, extension, blocks, sent, residual)


def residual_more_body(low, table, loads, extension, blocks, sent, residual):
    @pl.when(is_fine(table))
    def _():
        residual_rows(low, table, loads, extension, blocks, sent, residual)


def last_body(table, *refs):
    *pieces, correction, iterate, transfer, out, total, scratch, leaves = refs
    arrived, finals = pieces[: len(pieces) // 2], pieces[len(pieces) // 2 :]
    rows, _, width = total.shape
    copies = [
        pltpu.make_async_copy(total.at[i], out.at[:, pl.ds(i * width, width)], leaves.at[i])
        for i in range(rows)
    ]

    @pl.when(is_fine(table))
    def _():
        joined(arrived, scratch)
        for i in range(rows):
            value = iterate[i] + correction[i]
            total[i] = value + gathered(scratch, table, i, transfer)
            copies[i].start()

    @pl.when(jnp.logical_not(is_fine(table)))
    def _():
        for i in range(rows):
            total[i] = row_of(finals, i)
            copies[i].start()

    for copy in copies:
        copy.wait()


def local(loads, level_blocks, level_cols, smoother, transfer_blocks, transfer_cols, bound_rows):
    block_rows = level_cols.shape[1]
    width = level_blocks.shape[-1]
    load_cols = loads.shape[1]
    list_width = bound_rows.shape[-1]
    left_list, right_list, sibling_list = bound_rows[0, 0]
    blocks, smooth, transfer, loads = level_blocks[0], smoother[0], transfer_blocks[0], loads[0]

    def panels(count, kind):
        return jax.ShapeDtypeStruct((count, load_cols, width), kind)

    def held(count):
        return pltpu.VMEM((count, load_cols, width), jnp.bfloat16)

    wide, narrow = panels(block_rows, jnp.float32), panels(block_rows, jnp.bfloat16)
    bounds = [block_rows * share // 16 for share in SHARES]
    parts = list(zip(bounds[:-1], bounds[1:]))
    listed = panels(list_width, jnp.bfloat16)
    extended = panels(block_rows + 3 * list_width, jnp.bfloat16)
    rowwise = pltpu.SemaphoreType.DMA((block_rows,))

    load_panels, sent = call(
        open_body, (wide, narrow), inside(loads), in_specs=[HBM], scratch=[rowwise],
        cost=pl.CostEstimate(flops=5_000_000_000, bytes_accessed=2 * loads.size * 4, transcendentals=0),
    )
    arrived = [partner(sent, "level", 1)]

    def spread(values):
        return jnp.broadcast_to(values[:, None], (values.shape[0], LANES))

    def swap_both(odd, even):
        odd = swapped(odd, "dom", 1)
        even = even()
        even = swapped(even, "dom", 0)
        return even, odd

    def swap_beside(x):
        return partner(x, "level", 0)

    even = lax.axis_index("dom") % 2 == 0
    wanted_even, wanted_odd = swap_both(
        spread(jnp.where(even, left_list, right_list)), lambda: spread(jnp.where(even, right_list, left_list))
    )
    wanted_beside = swap_beside(spread(sibling_list))
    columns = level_cols.reshape(-1)
    from_left = (columns >= block_rows) & (columns < block_rows + list_width)
    from_right = (columns >= block_rows + list_width) & (columns < block_rows + 2 * list_width)
    moved = jnp.where(from_left, list_width, 0) - jnp.where(from_right, list_width, 0)
    columns = columns + jnp.where(even, moved, 0)
    fine = (lax.axis_index("level") < 2).astype(jnp.int32).reshape(1)

    level_table = spread(jnp.concatenate([columns, fine]))
    transfer_table = spread(jnp.concatenate([transfer_cols.reshape(-1), fine]))

    def fetched(source):
        return call(fetch_body, like(source), inside(loads), inside(source), in_specs=[HBM, HBM], scratch=[rowwise])

    def exchanged(bodies, fixed, pieces, rest, joins, scratch):
        listed_body, body = bodies

        def listed_rows(wanted, pieces, joins):
            each = len(pieces[0])
            return call(
                lambda *refs: listed_body(1, each, *refs), (listed,) + joins,
                *fixed, wanted, *sum(pieces, []), *rest, scratch=[held(list_width)] * scratch,
            )

        odd, *whole = listed_rows(wanted_odd, pieces, joins)
        whole = whole or sum(pieces, [])
        even, odd = swap_both(odd, lambda: listed_rows(wanted_even, [[x] for x in whole], ())[0])
        *results, beside = call(body, (wide, narrow, listed), *fixed, wanted_beside, *whole, *rest)
        return (*results, (even, odd, swap_beside(beside)))

    def in_parts(body, more_body, args, sources, rest, wanted):
        kept, passed = [], []
        for at, (low, high) in enumerate(parts):
            outs = (panels(high - low, jnp.bfloat16),) + (extended,) * (at == 0)
            outs += (panels(high - low, jnp.float32),) * wanted
            rounded, *more = call(
                lambda *refs: (more_body if at else body)(low, *refs), outs,
                *args, *sources, *rest,
            )
            if at == 0:
                sources = [more.pop(0)]
            kept += more
            passed.append(partner(rounded, "level", 1))
        return passed, kept, sources[0]

    transfer = fetched(transfer)
    residual, iterate = [load_panels], None
    for cycle_index in range(ITERS):
        if cycle_index > 0:
            arrived, residual, _ = in_parts(
                residual_start_body, residual_more_body, (level_table, load_panels),
                (rounded, *sides), (blocks,), True,
            )
        args, rest = (transfer_table, load_panels), (transfer, smooth)
        current, first, sides = exchanged(
            (first_listed_body, first_body), args, [residual, arrived], rest,
            (wide, narrow) if len(arrived) > 1 else (), True,
        )
        args = (level_table, current, first)
        ends = cycle_index + 1 == ITERS
        returned, finals, extension = in_parts(second_start_body, second_more_body, args, sides, (blocks, smooth), ends)
        correction = call(second_fine_body, wide, *args, extension, blocks, smooth, scratch=[held(block_rows)])
        if not ends:
            rest = [correction] + ([] if iterate is None else [iterate]) + [transfer]
            iterate, rounded, sides = exchanged(
                (update_listed_body, update_body), (transfer_table,), [returned], rest,
                (narrow,), False,
            )
    final = call(
        last_body, jax.ShapeDtypeStruct((load_cols, block_rows * width), jnp.float32),
        transfer_table, *returned, *finals, correction, iterate, transfer, out_specs=HBM,
        scratch=[pltpu.VMEM(wide.shape, jnp.float32), held(block_rows), rowwise],
    )
    return final[None]


def solution(mesh):
    in_specs = (
        P("level", None, "dom"),
        P("level", "dom", None, None, None),
        P("level", "dom", None),
        P("level", "dom", None, None),
        P("level", "dom", None, None, None),
        P("level", "dom", None),
        P("level", "dom", None, None),
    )
    out_specs = P("level", None, "dom")

    return jax.shard_map(local, mesh=mesh, in_specs=in_specs, out_specs=out_specs, check_vma=False)
```

```python
import jax
import jax.numpy as jnp
from jax import lax
from jax.experimental import pallas as pl
from jax.experimental.pallas import tpu as pltpu
from jax.sharding import PartitionSpec as P

ITERS = 2
LIMIT = 16 << 20
LANES = 128
VMEM = pl.BlockSpec(memory_space=pltpu.VMEM)
HBM = pl.BlockSpec(memory_space=pltpu.HBM)
NT = (((1,), (1,)), ((), ()))


def partner(x, axis, apart):
    return lax.ppermute(x, axis, [(i, i ^ 1 << apart) for i in range(lax.axis_size(axis))])


def swapped(x, axis, first):
    size = lax.axis_size(axis)
    pairs = [(i % size, (i + 1) % size) for i in range(first, first + size, 2)]
    return lax.ppermute(x, axis, pairs + [(b, a) for a, b in pairs])


def like(x):
    return jax.ShapeDtypeStruct(x.shape, x.dtype)


def inside(x):
    return pltpu.with_memory_space_constraint(x, pltpu.HBM)


def call(body, outs, *args, in_specs=None, out_specs=None, scratch=(), cost=None):
    if cost is None:
        size = sum(x.size * x.dtype.itemsize for x in (*args, *jax.tree.leaves(outs)))
        cost = pl.CostEstimate(flops=64 * size, bytes_accessed=size, transcendentals=0)
    return pl.pallas_call(
        body,
        out_shape=outs,
        in_specs=in_specs or [VMEM] * len(args),
        out_specs=out_specs or jax.tree.map(lambda _: VMEM, outs),
        scratch_shapes=list(scratch),
        cost_estimate=cost,
        compiler_params=pltpu.CompilerParams(vmem_limit_bytes=LIMIT),
    )(*args)


def entry(table, at):
    return table[pl.ds(at, 1), 0:1][0, 0]


def is_fine(table):
    return entry(table, table.shape[0] - 1) == 1


def times(panel, block):
    return lax.dot_general(panel, block, NT, preferred_element_type=jnp.float32)


def gathered(source, table, row, blocks):
    count = blocks.shape[1]
    left = jnp.concatenate([source[entry(table, row * count + k)] for k in range(count)], axis=1)
    right = jnp.concatenate([blocks[row, k] for k in range(count)], axis=1)
    return times(left, right)


def joined(parts, scratch):
    at = 0
    for part in parts:
        for i in range(part.shape[0]):
            scratch[at + i] = part[i]
        at += part.shape[0]


def panel_copies(loads, panels, arrivals):
    rows, _, width = panels.shape
    return [
        pltpu.make_async_copy(loads.at[:, pl.ds(i * width, width)], panels.at[i], arrivals.at[i])
        for i in range(rows)
    ]


def open_body(table, loads, sent, panels, arrivals):
    @pl.when(is_fine(table))
    def _():
        copies = panel_copies(loads, panels, arrivals)
        for copy in copies:
            copy.start()
        for i, copy in enumerate(copies):
            copy.wait()
            sent[i] = panels[i].astype(jnp.bfloat16)


def fetch_body(loads, source, panels, target, load_arrivals, arrivals):
    copies = panel_copies(loads, panels, load_arrivals)
    copies += [
        pltpu.make_async_copy(source.at[i], target.at[i], arrivals.at[i])
        for i in range(source.shape[0])
    ]
    for copy in copies:
        copy.start()
    for copy in copies:
        copy.wait()


def chosen(wanted, outs):
    return [(entry(rows, j), out, j) for rows, out in zip(wanted, outs) for j in range(out.shape[0])]


def first_listed_body(lists, pieces, table, loads, *refs):
    wanted, refs = refs[:lists], refs[lists:]
    residual, arrived, refs = refs[:pieces], refs[pieces : 2 * pieces], refs[2 * pieces :]
    transfer, smoother, *refs, scratch = refs
    outs = refs[:lists]
    places = chosen(wanted, outs)
    if pieces > 1:
        joined_residual, joined_arrived = refs[lists:]
    else:
        (joined_residual,), (joined_arrived,) = residual, arrived

    @pl.when(is_fine(table))
    def _():
        if pieces > 1:
            joined(residual, joined_residual)
        for at, (row, _, _) in enumerate(places):
            scratch[at] = joined_residual[row].astype(jnp.bfloat16)

    @pl.when(jnp.logical_not(is_fine(table)))
    def _():
        if pieces > 1:
            joined(arrived, joined_arrived)
        for at, (row, _, _) in enumerate(places):
            value = loads[row] + gathered(joined_arrived, table, row, transfer)
            scratch[at] = value.astype(jnp.bfloat16)

    for at, (row, out, j) in enumerate(places):
        out[j] = times(scratch[at], smoother[row]).astype(jnp.bfloat16)


def first_body(table, loads, wanted, residual, arrived, transfer, smoother, current, first, beside):
    rows = first.shape[0]

    @pl.when(is_fine(table))
    def _():
        joined([residual], current)

    @pl.when(jnp.logical_not(is_fine(table)))
    def _():
        for i in range(rows):
            current[i] = loads[i] + gathered(arrived, table, i, transfer)

    for i in range(rows):
        value = times(current[i].astype(jnp.bfloat16), smoother[i])
        first[i] = value.astype(jnp.bfloat16)
    for row, out, j in chosen([wanted], [beside]):
        out[j] = first[row]


def second_rows(low, table, current, first, extension, blocks, smoother, rounded, full=None):
    rows = rounded.shape[0]
    for i in range(rows):
        applied = gathered(extension, table, low + i, blocks)
        rounded[i] = (current[low + i] - applied).astype(jnp.bfloat16)
    for i in range(rows):
        value = first[low + i].astype(jnp.float32) + times(rounded[i], smoother[low + i])
        rounded[i] = value.astype(jnp.bfloat16)
        if full is not None:
            full[i] = value


def second_start_body(table, current, first, left, right, sibling, blocks, smoother, rounded, extension, *full):
    joined([first, left, right, sibling], extension)

    @pl.when(jnp.logical_not(is_fine(table)))
    def _():
        second_rows(0, table, current, first, extension, blocks, smoother, rounded, *full)


def second_end_body(table, current, first, extension, blocks, smoother, rounded, *full):
    @pl.when(jnp.logical_not(is_fine(table)))
    def _():
        low = first.shape[0] - rounded.shape[0]
        second_rows(low, table, current, first, extension, blocks, smoother, rounded, *full)


def second_fine_body(table, current, first, extension, blocks, smoother, full, scratch):
    @pl.when(is_fine(table))
    def _():
        second_rows(0, table, current, first, extension, blocks, smoother, scratch, full)


def row_of(parts, at):
    for part in parts:
        if at < part.shape[0]:
            return part[at]
        at -= part.shape[0]


def updated(row, arrived, table, transfer, correction, terms):
    value = correction[row]
    for term in terms:
        value = term[row] + value
    return value + gathered(arrived, table, row, transfer)


def update_listed_body(lists, pieces, table, *refs):
    wanted, arrived, refs = refs[:lists], refs[lists : lists + pieces], refs[lists + pieces :]
    more = lists + (pieces > 1)
    correction, *terms, transfer = refs[:-more]
    outs = refs[-more:][:lists]

    @pl.when(is_fine(table))
    def _():
        if pieces > 1:
            joined(arrived, refs[-1])
        source = refs[-1] if pieces > 1 else arrived[0]
        for row, out, j in chosen(wanted, outs):
            value = updated(row, source, table, transfer, correction, terms)
            out[j] = value.astype(jnp.bfloat16)


def update_body(table, wanted, arrived, correction, *refs):
    *terms, transfer, iterate, rounded, beside = refs

    @pl.when(is_fine(table))
    def _():
        for i in range(iterate.shape[0]):
            value = updated(i, arrived, table, transfer, correction, terms)
            iterate[i] = value
            rounded[i] = value.astype(jnp.bfloat16)
        for row, out, j in chosen([wanted], [beside]):
            out[j] = rounded[row]


def residual_body(low, table, loads, *refs):
    *sources, blocks, residual, sent = refs[: len(refs) - (low == 0)]

    @pl.when(is_fine(table))
    def _():
        if low == 0:
            extension = refs[-1]
            joined(sources, extension)
        else:
            (extension,) = sources
        for i in range(residual.shape[0]):
            value = loads[low + i] - gathered(extension, table, low + i, blocks)
            residual[i] = value
            sent[i] = value.astype(jnp.bfloat16)


def last_body(table, early, late, correction, start, end, iterate, transfer, out, total, scratch, leaves):
    rows, _, width = total.shape
    copies = [
        pltpu.make_async_copy(total.at[i], out.at[:, pl.ds(i * width, width)], leaves.at[i])
        for i in range(rows)
    ]

    @pl.when(is_fine(table))
    def _():
        joined((early, late), scratch)
        for i in range(rows):
            value = iterate[i] + correction[i]
            total[i] = value + gathered(scratch, table, i, transfer)
            copies[i].start()

    @pl.when(jnp.logical_not(is_fine(table)))
    def _():
        for i in range(rows):
            total[i] = row_of((start, end), i)
            copies[i].start()

    for copy in copies:
        copy.wait()


def local(loads, level_blocks, level_cols, smoother, transfer_blocks, transfer_cols, bound_rows):
    block_rows = level_cols.shape[1]
    width = level_blocks.shape[-1]
    load_cols = loads.shape[1]
    list_width = bound_rows.shape[-1]
    left_list, right_list, sibling_list = bound_rows[0, 0]
    blocks, smooth, transfer, loads = level_blocks[0], smoother[0], transfer_blocks[0], loads[0]

    def panels(count, kind):
        return jax.ShapeDtypeStruct((count, load_cols, width), kind)

    def held(count):
        return pltpu.VMEM((count, load_cols, width), jnp.bfloat16)

    wide, narrow = panels(block_rows, jnp.float32), panels(block_rows, jnp.bfloat16)
    early_rows = block_rows * 5 // 8
    late_rows = block_rows - early_rows
    listed = panels(list_width, jnp.bfloat16)
    extended = panels(block_rows + 3 * list_width, jnp.bfloat16)
    rowwise = pltpu.SemaphoreType.DMA((block_rows,))

    fine = (lax.axis_index("level") < 2).astype(jnp.int32).reshape(1)
    sent = call(
        open_body, narrow, jnp.broadcast_to(fine[:, None], (1, LANES)), inside(loads),
        in_specs=[VMEM, HBM], scratch=[pltpu.VMEM(wide.shape, jnp.float32), rowwise],
        cost=pl.CostEstimate(flops=5_000_000_000, bytes_accessed=2 * loads.size * 4, transcendentals=0),
    )
    arrived = [partner(sent, "level", 1)]

    def spread(values):
        return jnp.broadcast_to(values[:, None], (values.shape[0], LANES))

    def swap_both(odd, even):
        odd = swapped(odd, "dom", 1)
        even = swapped(even, "dom", 0)
        return even, odd

    def swap_beside(x):
        return partner(x, "level", 0)

    even = lax.axis_index("dom") % 2 == 0
    wanted_even, wanted_odd = swap_both(
        spread(jnp.where(even, left_list, right_list)), spread(jnp.where(even, right_list, left_list))
    )
    wanted_beside = swap_beside(spread(sibling_list))
    columns = level_cols.reshape(-1)
    from_left = (columns >= block_rows) & (columns < block_rows + list_width)
    from_right = (columns >= block_rows + list_width) & (columns < block_rows + 2 * list_width)
    moved = jnp.where(from_left, list_width, 0) - jnp.where(from_right, list_width, 0)
    columns = columns + jnp.where(even, moved, 0)

    level_table = spread(jnp.concatenate([columns, fine]))
    transfer_table = spread(jnp.concatenate([transfer_cols.reshape(-1), fine]))

    def exchanged(bodies, fixed, pieces, rest, joins, scratch):
        listed_body, body = bodies
        each = len(pieces[0])
        odd, even, *whole = call(
            lambda *refs: listed_body(2, each, *refs), (listed,) * 2 + joins,
            *fixed, wanted_odd, wanted_even, *sum(pieces, []), *rest,
            scratch=[held(2 * list_width)] * scratch,
        )
        even, odd = swap_both(odd, even)
        whole = whole or sum(pieces, [])
        *results, beside = call(body, (wide, narrow, listed), *fixed, wanted_beside, *whole, *rest)
        return (*results, (even, odd, swap_beside(beside)))

    def part(rows):
        return panels(rows, jnp.float32), panels(rows, jnp.bfloat16)

    def sent_on(x):
        return partner(x, "level", 1)

    load_panels, transfer = call(
        fetch_body, (wide, like(transfer)), inside(loads), inside(transfer),
        in_specs=[HBM, HBM], scratch=[rowwise, rowwise],
    )
    residual, iterate = [load_panels], None
    for cycle_index in range(ITERS):
        if cycle_index > 0:
            args = (level_table, load_panels)
            early, sent, extension = call(
                lambda *refs: residual_body(0, *refs), part(early_rows) + (extended,),
                *args, rounded, *sides, blocks,
            )
            arrived = [sent_on(sent)]
            late, sent = call(
                lambda *refs: residual_body(early_rows, *refs), part(late_rows),
                *args, extension, blocks,
            )
            arrived.append(partner(sent, "level", 1))
            residual = [early, late]
        args, rest = (transfer_table, load_panels), (transfer, smooth)
        current, first, sides = exchanged(
            (first_listed_body, first_body), args, [residual, arrived], rest,
            (wide, narrow) if len(arrived) > 1 else (), True,
        )
        args = (level_table, current, first)
        ends = cycle_index + 1 == ITERS
        rounded, extension, *start = call(
            second_start_body,
            (panels(early_rows, jnp.bfloat16), extended) + (panels(early_rows, jnp.float32),) * ends,
            *args, *sides, blocks, smooth,
        )
        returned = [sent_on(rounded)]
        rounded, *end = call(
            second_end_body,
            (panels(late_rows, jnp.bfloat16),) + (panels(late_rows, jnp.float32),) * ends,
            *args, extension, blocks, smooth,
        )
        returned.append(sent_on(rounded))
        correction = call(second_fine_body, wide, *args, extension, blocks, smooth, scratch=[held(block_rows)])
        if not ends:
            rest = [correction] + ([] if iterate is None else [iterate]) + [transfer]
            iterate, rounded, sides = exchanged(
                (update_listed_body, update_body), (transfer_table,), [returned], rest,
                (narrow,), False,
            )
    final = call(
        last_body, jax.ShapeDtypeStruct((load_cols, block_rows * width), jnp.float32),
        transfer_table, *returned, correction, *start, *end, iterate, transfer, out_specs=HBM,
        scratch=[pltpu.VMEM(wide.shape, jnp.float32), held(block_rows), rowwise],
    )
    return final[None]


def solution(mesh):
    in_specs = (
        P("level", None, "dom"),
        P("level", "dom", None, None, None),
        P("level", "dom", None),
        P("level", "dom", None, None),
        P("level", "dom", None, None, None),
        P("level", "dom", None),
        P("level", "dom", None, None),
    )
    out_specs = P("level", None, "dom")

    return jax.shard_map(local, mesh=mesh, in_specs=in_specs, out_specs=out_specs, check_vma=False)
```
